256 devices in a mesh: orow: 16 (over z_lo, x), ocol: 16 (over z_hi, y, core).
Axes of the slice: x: 4, y: 4, z: 8 (z_hi: 2, z_lo: 4; z = z_hi * 4 + z_lo), core: 2. Of those that a mesh axis runs over, the one named last changes fastest.
Arguments:
- amplitudes: bfloat16 [16, 16, 512, 512], P('orow', 'ocol'), may hold values from -6 to 6
- tile_mask: int32 [16, 16, 2, 2], P('orow', 'ocol'), may hold values 0 or 1
- domain_tiles: int32 [16, 16, 2], replicated, may hold values from 0 to 7, as said below
- cholesky: bfloat16 [16, 2048, 2048], P('ocol'), as said below
Outputs:
- ladder_sym: float32 [16, 16, 512, 512], P('orow', 'ocol')
The draws below stay inside these ranges and needn't reach their ends.
Inputs may be any that keep to these rules, and one draw needn't show every extreme that they name: `domain_tiles`: for every pair the 2 tile numbers differ, and pair (j, i) lists the same tiles in the same order as pair (i, j). Every vector cholesky[q] is a symmetric 2048 x 2048 matrix.
All inputs are finite; a program needn't handle non-finite values. No bound on the sum of `tile_mask` on one device may be relied on, other than what follows from the above.
Results may differ from the reference program's by a relative error of at most 0.0029.
Values may be sent and summed in bfloat16 or wider, within the bound.
A program may use at most 128 MiB of HBM per device.

```python
import jax
import jax.numpy as jnp
from jax import lax

TILE = 256
NT = 8
K = 2
NO = 16
NQ = 16
V = 2048
DV = 512


def draw_domain_tiles(key, part):
    first_key, second_key = jax.random.split(jax.random.fold_in(key, 7))
    first = jax.random.randint(first_key, (NO, NO), 0, NT)
    offset = jax.random.randint(second_key, (NO, NO), 1, NT)
    second = (first + offset) % NT
    both = jnp.stack([first, second], axis=-1).astype(jnp.int32)
    rows = jnp.arange(NO, dtype=jnp.int32)[:, None, None]
    cols = jnp.arange(NO, dtype=jnp.int32)[None, :, None]
    return jnp.where(rows <= cols, both, both.transpose(1, 0, 2)).astype(jnp.int32)


def draw_cholesky(key, part):
    sub_key = jax.random.fold_in(key, 11)
    spread = (2.0 / (4.0 * DV)) ** 0.5
    raw = jnp.clip(jax.random.normal(sub_key, (NQ, V, V), jnp.float32), -6.0, 6.0)
    mirrored = (raw + raw.transpose(0, 2, 1)) * (0.5 * spread)
    return mirrored.astype(jnp.bfloat16)


def place_ends(entries, stream_key, least, high):
    place = [jax.random.randint(jax.random.fold_in(stream_key, axis), (), 0, length) for axis, length in enumerate(entries.shape)]
    main_axis = entries.shape.index(max(entries.shape))
    neighbour = place[:main_axis] + [(place[main_axis] + 1) % entries.shape[main_axis]] + place[main_axis + 1:]
    return entries.at[tuple(place)].set(least).at[tuple(neighbour)].set(high)


def level_of(stream_key, extent, cuts, low, top_value):
    loudness, own = 1.0, jax.random.fold_in(stream_key, 6)
    for dim, shards_of in cuts:
        heights = jnp.exp(jax.random.uniform(jax.random.fold_in(own, dim), (shards_of,), jnp.float32, low / len(cuts), top_value / len(cuts)))
        loudness = loudness * jnp.repeat(heights, extent[dim] // shards_of).reshape([-1 if axis == dim else 1 for axis in range(len(extent))])
    return loudness


def bell_draw(key, extent, scale, limit, shards=(), kind=jnp.bfloat16):
    factor_of = level_of(key, extent, shards, -0.22, 0.18) if shards else 1.0
    array = jax.random.normal(key, extent, jnp.float32) * scale * factor_of
    return jnp.minimum(jnp.maximum(array, -limit), limit).astype(kind)


def setup_inputs(seed: int = 0) -> dict:
    key_list = jax.random.split(jax.random.key(seed), 5)
    return {
        "amplitudes": bell_draw(key_list[0], (NO, NO, DV, DV), 1.0, 6.0, ((0, 16), (1, 16))),
        "tile_mask": place_ends((jax.random.randint(key_list[1], (NO, NO, K, K), 0, 4) < 3).astype(jnp.int32), jax.random.fold_in(key_list[1], 1), 0, 1),
        "domain_tiles": draw_domain_tiles(jax.random.fold_in(key_list[4], 71), 0),
        "cholesky": draw_cholesky(jax.random.fold_in(key_list[4], 71), 0),
    }


def pick_tiles(factor_all, chosen):
    number = factor_all.shape[0]
    tiles = factor_all.shape[1] // TILE
    blocked = factor_all.reshape(number, tiles, TILE, tiles, TILE)
    picked = blocked[:, chosen[:, None], :, chosen[None, :], :]
    width = chosen.shape[0] * TILE
    return picked.transpose(2, 0, 3, 1, 4).reshape(number, width, width)


def reference(amplitudes, tile_mask, domain_tiles, cholesky):
    def one_pair(flat_index):
        row_index = flat_index // NO
        col_index = flat_index % NO
        sub_factor = pick_tiles(cholesky, domain_tiles[row_index, col_index])
        shaped = amplitudes[row_index, col_index].reshape(K, TILE, K, TILE)
        weights = tile_mask[row_index, col_index].astype(jnp.bfloat16)[:, None, :, None]
        weighted = (shaped * weights).reshape(K * TILE, K * TILE)
        inner = jnp.einsum("qac,cd->qad", sub_factor.astype(jnp.float32), weighted.astype(jnp.float32)).astype(jnp.bfloat16)
        return jnp.einsum("qad,qbd->ab", inner.astype(jnp.float32), sub_factor.astype(jnp.float32))

    flat = lax.map(one_pair, jnp.arange(NO * NO, dtype=jnp.int32))
    ladder = flat.reshape(NO, NO, K * TILE, K * TILE)
    return ladder + ladder.transpose(1, 0, 3, 2)
```

```python
import functools

import jax
import jax.numpy as jnp
from jax import lax
from jax.experimental import pallas as pl
from jax.experimental.pallas import tpu as pltpu
from jax.sharding import PartitionSpec as P

TILE = 256
DV = 512
NO = 16
RING = 8
PARTS = ((0, 0), (0, 1), (1, 1))
CHUNKS = 4
ROWS = DV // CHUNKS
MESH = pl.DeviceIdType.MESH


def flip(index):
    return index + RING - 2 * RING * (index // RING)


def prep_kernel(tiles_ref, mask_ref, amp_ref, chol_ref, pack_ref, weighted_ref, sems):
    i = lax.axis_index("orow")
    half = lax.axis_index("ocol") // RING
    copies = []
    for s in range(RING + 1):
        if s < RING:
            j = half * RING + s
            other = jnp.logical_and(i // RING == half, i > j)
            a = jnp.where(other, flip(i), i)
            b = jnp.where(other, flip(j), j)
        else:
            a = b = flip(i)
        picks = (tiles_ref[a, b, 0], tiles_ref[a, b, 1])
        for k, (r, c) in enumerate(PARTS):
            copy = pltpu.make_async_copy(
                chol_ref.at[
                    0,
                    pl.ds(pl.multiple_of(picks[r] * TILE, TILE), TILE),
                    pl.ds(pl.multiple_of(picks[c] * TILE, TILE), TILE),
                ],
                pack_ref.at[s, k],
                sems.at[s * 3 + k],
            )
            copy.start()
            copies.append(copy)
    for s in range(2):
        for t in range(2):
            block = (pl.ds(s * TILE, TILE), pl.ds(t * TILE, TILE))
            keep = mask_ref[0, 0, s, t].astype(jnp.float32).astype(jnp.bfloat16)
            weighted_ref[block] = amp_ref[(0, 0) + block] * keep
    for copy in copies:
        copy.wait()


def ladder_kernel(
    pack_ref, weighted_ref, out_ref,
    slots, extra, factor, inputs, inner, total, give, give_more, got, got_more,
    f_send, f_recv, x_send, x_recv, w_send, w_recv, p_send, p_recv, m_send, m_recv,
):
    i = lax.axis_index("orow")
    j = lax.axis_index("ocol")
    half = j // RING
    me = j - half * RING
    y, core = me // 2, me % 2
    fi, fj = flip(i), flip(j)
    same = i // RING == half
    diag = i == j
    lower = jnp.logical_and(same, i > j)
    upper = jnp.logical_and(same, i < j)
    swapped = jnp.logical_and(same, i <= j)
    dflag = jnp.where(diag, 1, 0)
    w_dev = (jnp.where(swapped, fj, j), jnp.where(swapped, fi, i))
    p_swap = jnp.logical_or(lower, diag)
    p_dev = (jnp.where(p_swap, fj, j), jnp.where(p_swap, fi, i))
    m_dev = (fi, fj)

    def peer(k):
        step = k // 2
        dy = step + step // 2 - 2 * (step // 3)
        return ((y + dy) % 4) * 2 + (core + k) % 2

    barrier = pltpu.get_barrier_semaphore()

    def greet(device):
        pl.semaphore_signal(barrier, inc=1, device_id=device, device_id_type=MESH)

    for k in range(1, RING):
        greet((i, half * RING + peer(k)))
    greet(w_dev)

    @pl.when(jnp.logical_or(upper, lower))
    def _():
        greet(p_dev)

    @pl.when(lower)
    def _():
        greet(m_dev)

    pl.semaphore_wait(barrier, RING + jnp.where(i == j, 0, jnp.where(same, 1, 0)) + jnp.where(lower, 1, 0))

    def remote(src, dst, send, recv, device):
        return pltpu.make_async_remote_copy(
            src_ref=src, dst_ref=dst, send_sem=send, recv_sem=recv, device_id=device, device_id_type=MESH
        )

    w_copy = remote(weighted_ref, inputs.at[1], w_send.at[1], w_recv.at[1], w_dev)
    w_more = remote(weighted_ref, inputs.at[0], w_send.at[0], w_recv.at[0], m_dev)
    w_own = pltpu.make_async_copy(weighted_ref, inputs.at[0], w_recv.at[0])
    w_copy.start()

    @pl.when(lower)
    def _():
        w_more.start()

    @pl.when(jnp.logical_not(lower))
    def _():
        w_own.start()

    def f_copy(k):
        to = peer(k)
        return remote(pack_ref.at[to], slots.at[me], f_send.at[k], f_recv.at[me], (i, half * RING + to))

    f_own = pltpu.make_async_copy(pack_ref.at[me], slots.at[me], f_send.at[0])
    f_own.start()
    x_copy = remote(pack_ref.at[RING], extra.at[me], x_send.at[0], x_recv.at[me], (i, i))
    x_own = pltpu.make_async_copy(pack_ref.at[RING], extra.at[me], x_send.at[1])
    for k in range(1, RING):
        f_copy(k).start()

    @pl.when(jnp.logical_and(same, jnp.logical_not(diag)))
    def _():
        x_copy.start()

    @pl.when(diag)
    def _():
        x_own.start()

    total[...] = jnp.zeros_like(total)
    w_copy.wait_recv()

    @pl.when(lower)
    def _():
        w_more.wait_recv()

    @pl.when(jnp.logical_not(lower))
    def _():
        w_own.wait()

    f_own.wait()

    @pl.when(diag)
    def _():
        x_own.wait()

    def build(source, slot, which):
        factor[which, :TILE, :TILE] = source[slot, 0]
        factor[which, :TILE, TILE:] = source[slot, 1]
        factor[which, TILE:, :TILE] = source[slot, 1].T
        factor[which, TILE:, TILE:] = source[slot, 2]

    def add(side, which):
        for c in range(2):
            cols = pl.ds(c * TILE, TILE)
            inner[:, cols] = jnp.dot(
                factor[which], inputs[side, :, cols], preferred_element_type=jnp.float32
            ).astype(jnp.bfloat16)
        for c in range(2):
            cols = pl.ds(c * TILE, TILE)
            total[side, :, cols] += jnp.dot(
                inner[...], factor[which, :, cols], preferred_element_type=jnp.float32
            )

    def step(k, carry):
        slot = peer(k)

        @pl.when(k > 0)
        def _():
            remote(pack_ref.at[slot], slots.at[slot], f_send.at[slot], f_recv.at[slot], w_dev).wait_recv()

        build(slots, slot, 0)

        @pl.when(diag)
        def _():
            @pl.when(k > 0)
            def _():
                remote(pack_ref.at[RING], extra.at[slot], x_send.at[0], x_recv.at[slot], w_dev).wait_recv()

            build(extra, slot, 1)

        add(0, 0)
        add(1, dflag)
        return carry

    lax.fori_loop(0, RING, step, 0)

    def p_copy(r):
        return remote(give.at[r], got.at[r], p_send.at[r], p_recv.at[r], p_dev)

    def m_copy(r):
        return remote(give_more.at[r], got_more.at[r], m_send.at[r], m_recv.at[r], m_dev)

    for r in range(CHUNKS):
        rows = pl.ds(r * ROWS, ROWS)
        give[r] = (total[1, rows, :] + total[dflag, :, rows].T).astype(jnp.bfloat16)
        p_copy(r).start()
        own = total[0, rows, :] + total[1 - dflag, :, rows].T
        out_ref[rows, :] = own

        @pl.when(lower)
        def _():
            give_more[r] = own.astype(jnp.bfloat16)
            m_copy(r).start()

    for r in range(CHUNKS):
        rows = pl.ds(r * ROWS, ROWS)
        p_copy(r).wait_recv()

        @pl.when(lower)
        def _():
            m_copy(r).wait_recv()
            out_ref[rows, :] = got[r].astype(jnp.float32) + got_more[r].astype(jnp.float32)

        @pl.when(jnp.logical_not(lower))
        def _():
            out_ref[rows, :] += got[r].astype(jnp.float32)

    w_copy.wait_send()
    for k in range(1, RING):
        f_copy(k).wait_send()
    for r in range(CHUNKS):
        p_copy(r).wait_send()

    @pl.when(jnp.logical_and(same, jnp.logical_not(diag)))
    def _():
        x_copy.wait_send()

    @pl.when(lower)
    def _():
        w_more.wait_send()
        for r in range(CHUNKS):
            m_copy(r).wait_send()


def shards(amplitudes, tile_mask, domain_tiles, cholesky):
    vmem = pl.BlockSpec(memory_space=pltpu.VMEM)
    smem = pl.BlockSpec(memory_space=pltpu.SMEM)
    dma = pltpu.SemaphoreType.DMA
    half = jnp.bfloat16
    pack, weighted = pl.pallas_call(
        prep_kernel,
        out_shape=(
            pltpu.VMEM((RING + 1, 3, TILE, TILE), half),
            pltpu.VMEM((DV, DV), half),
        ),
        in_specs=[smem, smem, vmem, pl.BlockSpec(memory_space=pl.ANY)],
        out_specs=(vmem, vmem),
        scratch_shapes=[dma((3 * RING + 3,))],
        compiler_params=pltpu.CompilerParams(vmem_limit_bytes=56 << 20),
        name="prep",
    )(domain_tiles, tile_mask, amplitudes, cholesky)
    ladder = pl.pallas_call(
        ladder_kernel,
        out_shape=jax.ShapeDtypeStruct((DV, DV), jnp.float32),
        in_specs=[vmem, vmem],
        out_specs=vmem,
        scratch_shapes=[
            pltpu.VMEM((RING, 3, TILE, TILE), half),
            pltpu.VMEM((RING, 3, TILE, TILE), half),
            pltpu.VMEM((2, DV, DV), half),
            pltpu.VMEM((2, DV, DV), half),
            pltpu.VMEM((DV, DV), half),
            pltpu.VMEM((2, DV, DV), jnp.float32),
            pltpu.VMEM((CHUNKS, ROWS, DV), half),
            pltpu.VMEM((CHUNKS, ROWS, DV), half),
            pltpu.VMEM((CHUNKS, ROWS, DV), half),
            pltpu.VMEM((CHUNKS, ROWS, DV), half),
            dma((RING,)), dma((RING,)), dma((2,)), dma((RING,)), dma((2,)), dma((2,)),
            dma((CHUNKS,)), dma((CHUNKS,)), dma((CHUNKS,)), dma((CHUNKS,)),
        ],
        compiler_params=pltpu.CompilerParams(
            collective_id=0, has_side_effects=True, vmem_limit_bytes=36 << 20
        ),
        name="ladder",
    )(pack, weighted)
    return ladder.reshape(1, 1, DV, DV)


def solution(mesh):
    return jax.shard_map(
        shards,
        mesh=mesh,
        in_specs=(
            P("orow", "ocol", None, None),
            P("orow", "ocol", None, None),
            P(),
            P("ocol", None, None),
        ),
        out_specs=P("orow", "ocol", None, None),
        check_vma=False,
    )
```

```python
import jax
import jax.numpy as jnp
from jax import lax
from jax.experimental import pallas as pl
from jax.experimental.pallas import tpu as pltpu
from jax.sharding import PartitionSpec as P

TILE = 256
HT = 128
DV = 512
NO = 16
RING = 8
CHUNKS = 4
ROWS = DV // CHUNKS
PACK = 8 * HT + 16
MESH = pl.DeviceIdType.MESH


def flip(index):
    return index + RING - 2 * RING * (index // RING)


def corner(shape=(HT, HT)):
    return lax.broadcasted_iota(jnp.int32, shape, 0), lax.broadcasted_iota(jnp.int32, shape, 1)


def prep_kernel(tiles_ref, mask_ref, amp_ref, chol_ref, pack_ref, weighted_ref, stage, raw, sems, raw_sem):
    i = lax.axis_index("orow")
    half = lax.axis_index("ocol") // RING
    raw_copy = pltpu.make_async_copy(amp_ref, raw, raw_sem)
    copies = []
    for s in range(RING + 1):
        if s < RING:
            j = half * RING + s
            other = jnp.logical_and(i // RING == half, i > j)
            a = jnp.where(other, flip(i), i)
            b = jnp.where(other, flip(j), j)
        else:
            a = b = flip(i)
        t0 = tiles_ref[a, 0, b] * TILE
        t1 = tiles_ref[a, 1, b] * TILE

        def pick(row, col, height, dst, sem):
            copy = pltpu.make_async_copy(
                chol_ref.at[0, pl.ds(pl.multiple_of(row, HT), height), pl.ds(pl.multiple_of(col, HT), HT)], dst, sem
            )
            copy.start()
            return copy

        mine = []
        for n, (t, off) in enumerate(((t0, 0), (t0, HT), (t1, 0), (t1, HT))):
            mine.append(pick(t + off, t + off, HT, stage.at[s, n], sems.at[s, n]))
        for n, (row, col, height, at) in enumerate(
            ((t0, t1, TILE, 0), (t0, t1 + HT, TILE, TILE), (t0, t0 + HT, HT, 2 * TILE), (t1, t1 + HT, HT, 2 * TILE + HT))
        ):
            mine.append(pick(row, col, height, pack_ref.at[s, pl.ds(at, height)], sems.at[s, 4 + n]))
        copies.append(mine)
        if s == 0:
            raw_copy.start()
    row, col = corner()
    line = lax.broadcasted_iota(jnp.int32, (16, HT), 0)
    raw_copy.wait()
    for s in range(2):
        for t in range(2):
            keep = mask_ref[0, 0, s, t].astype(jnp.float32).astype(jnp.bfloat16)
            weighted_ref[t, pl.ds(s * TILE, TILE), :] = raw[0, 0, pl.ds(s * TILE, TILE), pl.ds(t * TILE, TILE)] * keep
    for s in range(RING + 1):
        for n in range(4):
            copies[s][n].wait()
        blocks = [stage[s, n].astype(jnp.float32) for n in range(4)]
        pack_ref[s, 6 * HT : 7 * HT, :] = jnp.where(row <= col, blocks[0], blocks[1]).astype(jnp.bfloat16)
        pack_ref[s, 7 * HT : 8 * HT, :] = jnp.where(row <= col, blocks[2], blocks[3]).astype(jnp.bfloat16)
        ends = [jnp.sum(jnp.where(row == col, blocks[n], 0.0), axis=0, keepdims=True) for n in (1, 3)]
        pack_ref[s, 8 * HT :, :] = jnp.where(line == 0, ends[0], ends[1]).astype(jnp.bfloat16)
    for s in range(RING + 1):
        for n in range(4, 8):
            copies[s][n].wait()


def ladder_kernel(
    pack_ref, weighted_ref, out_ref,
    slots, extra, factor, inputs, inner, total, give, got, pass_on, passed,
    f_send, f_recv, x_send, x_recv, w_send, w_recv, p_send, p_recv, m_send, m_recv,
):
    i = lax.axis_index("orow")
    j = lax.axis_index("ocol")
    half = j // RING
    me = j - half * RING
    y, core = me // 2, me % 2
    fi, fj = flip(i), flip(j)
    same = i // RING == half
    diag = i == j
    lower = jnp.logical_and(same, i > j)
    upper = jnp.logical_and(same, i < j)
    not_lower = jnp.logical_not(lower)
    not_upper = jnp.logical_not(upper)
    swapped = jnp.logical_and(same, i <= j)
    dflag = jnp.where(diag, 1, 0)
    w_dev = (jnp.where(swapped, fj, j), jnp.where(swapped, fi, i))
    p_swap = jnp.logical_or(lower, diag)
    p_dev = (jnp.where(p_swap, fj, j), jnp.where(p_swap, fi, i))
    m_dev = (fi, fj)
    t_dev = (j, i)

    def peer(k):
        step = k // 2
        dy = step + step // 2 - 2 * (step // 3)
        return ((y + dy) % 4) * 2 + (core + k) % 2

    barrier = pltpu.get_barrier_semaphore()

    def greet(device):
        pl.semaphore_signal(barrier, inc=1, device_id=device, device_id_type=MESH)

    for k in range(1, RING):
        greet((i, half * RING + peer(k)))
    greet(w_dev)

    @pl.when(jnp.logical_or(upper, lower))
    def _():
        greet(p_dev)

    @pl.when(lower)
    def _():
        greet(m_dev)

    pl.semaphore_wait(barrier, RING + jnp.where(diag, 0, jnp.where(same, 1, 0)) + jnp.where(lower, 1, 0))

    def remote(src, dst, send, recv, device):
        return pltpu.make_async_remote_copy(
            src_ref=src, dst_ref=dst, send_sem=send, recv_sem=recv, device_id=device, device_id_type=MESH
        )

    def w_copy(h):
        return remote(weighted_ref.at[h], inputs.at[1, h], w_send.at[1, h], w_recv.at[1, h], w_dev)

    def w_more(h):
        return remote(weighted_ref.at[h], inputs.at[0, h], w_send.at[0, h], w_recv.at[0, h], m_dev)

    def w_own(h):
        return pltpu.make_async_copy(weighted_ref.at[h], inputs.at[0, h], w_recv.at[0, h])

    for h in range(2):
        w_copy(h).start()

        @pl.when(lower)
        def _():
            w_more(h).start()

        @pl.when(not_lower)
        def _():
            w_own(h).start()

    def f_copy(k):
        to = peer(k)
        return remote(pack_ref.at[to], slots.at[me], f_send.at[k], f_recv.at[me], (i, half * RING + to))

    f_own = pltpu.make_async_copy(pack_ref.at[me], slots.at[me], f_send.at[0])
    f_own.start()
    x_copy = remote(pack_ref.at[RING], extra.at[me], x_send.at[0], x_recv.at[me], (i, i))
    x_own = pltpu.make_async_copy(pack_ref.at[RING], extra.at[me], x_send.at[1])
    for k in range(1, RING):
        f_copy(k).start()

    @pl.when(jnp.logical_and(same, jnp.logical_not(diag)))
    def _():
        x_copy.start()

    @pl.when(diag)
    def _():
        x_own.start()

    total[...] = jnp.zeros_like(total)

    @pl.when(not_lower)
    def _():
        for h in range(2):
            w_own(h).wait()

    f_own.wait()

    @pl.when(diag)
    def _():
        x_own.wait()

    row, col = corner()

    def build(source, slot, which):
        for n in range(2):
            at = n * TILE
            side = source[slot, 4 * HT + n * HT : 5 * HT + n * HT, :]
            mixed = source[slot, 6 * HT + n * HT : 7 * HT + n * HT, :].astype(jnp.float32)
            turned = mixed.T
            ends = source[slot, 8 * HT :, :].astype(jnp.float32)[n : n + 1, :]
            factor[which, at : at + HT, at : at + HT] = jnp.where(row <= col, mixed, turned).astype(jnp.bfloat16)
            factor[which, at : at + HT, at + HT : at + TILE] = side
            factor[which, at + HT : at + TILE, at : at + HT] = side.T
            factor[which, at + HT : at + TILE, at + HT : at + TILE] = jnp.where(
                row > col, mixed, jnp.where(row == col, ends, turned)
            ).astype(jnp.bfloat16)
            block = source[slot, n * TILE : n * TILE + TILE, :]
            factor[which, :TILE, TILE + n * HT : TILE + n * HT + HT] = block
            factor[which, TILE + n * HT : TILE + n * HT + HT, :TILE] = block.T

    def add(side, h, which):
        inner[...] = jnp.dot(factor[which], inputs[side, h], preferred_element_type=jnp.float32).astype(jnp.bfloat16)
        for c in range(2):
            cols = pl.ds(c * TILE, TILE)
            total[side, :, cols] += jnp.dot(
                inner[...], factor[which, h * TILE : h * TILE + TILE, cols], preferred_element_type=jnp.float32
            )

    def add_remote(h, slot):
        add(1, h, slot + RING * dflag)

        @pl.when(lower)
        def _():
            add(0, h, slot)

    def await_inputs(h):
        w_copy(h).wait_recv()

        @pl.when(lower)
        def _():
            w_more(h).wait_recv()

    def arrive(k):
        slot = peer(k)

        @pl.when(k > 0)
        def _():
            remote(pack_ref.at[slot], slots.at[slot], f_send.at[slot], f_recv.at[slot], w_dev).wait_recv()

        build(slots, slot, slot)

        @pl.when(diag)
        def _():
            @pl.when(k > 0)
            def _():
                remote(pack_ref.at[RING], extra.at[slot], x_send.at[0], x_recv.at[slot], w_dev).wait_recv()

            build(extra, slot, slot + RING)

        @pl.when(not_lower)
        def _():
            add(0, 0, slot)
            add(0, 1, slot)

    def first(k, carry):
        arrive(k)

        @pl.when(k == RING // 2)
        def _():
            await_inputs(0)

        @pl.when(k >= RING // 2)
        def _():
            def again(n, carry):
                add_remote(0, peer(k - n * (RING // 2)))
                return carry

            lax.fori_loop(0, 2, again, 0)

        return carry

    lax.fori_loop(0, RING, first, 0)
    await_inputs(1)

    def second(k, carry):
        add_remote(1, k)
        return carry

    lax.fori_loop(0, RING, second, 0)

    def p_copy(r):
        return remote(give.at[r], got.at[r], p_send.at[r], p_recv.at[r], p_dev)

    def m_copy(r):
        return remote(pass_on.at[r], passed.at[r], m_send.at[r], m_recv.at[r], t_dev)

    @pl.when(not_upper)
    def _():
        for r in range(CHUNKS):
            rows = pl.ds(r * ROWS, ROWS)
            give[r] = (total[1, rows, :] + total[dflag, :, rows].T).astype(jnp.bfloat16)
            p_copy(r).start()

    @pl.when(not_lower)
    def _():
        for r in range(CHUNKS):
            rows = pl.ds(r * ROWS, ROWS)
            out_ref[rows, :] = total[0, rows, :] + total[1 - dflag, :, rows].T
        for r in range(CHUNKS):
            rows = pl.ds(r * ROWS, ROWS)
            p_copy(r).wait_recv()
            ours = out_ref[rows, :] + got[r].astype(jnp.float32)
            out_ref[rows, :] = ours

            @pl.when(upper)
            def _():
                pass_on[r] = ours.astype(jnp.bfloat16)
                m_copy(r).start()

    @pl.when(lower)
    def _():
        for r in range(CHUNKS):
            m_copy(r).wait_recv()
            out_ref[:, pl.ds(r * ROWS, ROWS)] = passed[r].astype(jnp.float32).T

    for h in range(2):
        w_copy(h).wait_send()
    for k in range(1, RING):
        f_copy(k).wait_send()

    @pl.when(not_upper)
    def _():
        for r in range(CHUNKS):
            p_copy(r).wait_send()

    @pl.when(upper)
    def _():
        for r in range(CHUNKS):
            m_copy(r).wait_send()

    @pl.when(jnp.logical_and(same, jnp.logical_not(diag)))
    def _():
        x_copy.wait_send()

    @pl.when(lower)
    def _():
        for h in range(2):
            w_more(h).wait_send()


def shards(amplitudes, tile_mask, domain_tiles, cholesky):
    vmem = pl.BlockSpec(memory_space=pltpu.VMEM)
    smem = pl.BlockSpec(memory_space=pltpu.SMEM)
    hbm = pl.BlockSpec(memory_space=pl.ANY)
    dma = pltpu.SemaphoreType.DMA
    half = jnp.bfloat16
    pack, weighted = pl.pallas_call(
        prep_kernel,
        out_shape=(
            pltpu.VMEM((RING + 1, PACK, HT), half),
            pltpu.VMEM((2, DV, TILE), half),
        ),
        in_specs=[smem, smem, hbm, hbm],
        out_specs=(vmem, vmem),
        scratch_shapes=[
            pltpu.VMEM((RING + 1, 4, HT, HT), half),
            pltpu.VMEM((1, 1, DV, DV), half),
            dma((RING + 1, 8)),
            dma,
        ],
        compiler_params=pltpu.CompilerParams(vmem_limit_bytes=56 << 20),
        name="prep",
    )(domain_tiles.transpose(0, 2, 1), tile_mask, amplitudes, cholesky)
    ladder = pl.pallas_call(
        ladder_kernel,
        out_shape=jax.ShapeDtypeStruct((DV, DV), jnp.float32),
        in_specs=[vmem, vmem],
        out_specs=vmem,
        scratch_shapes=[
            pltpu.VMEM((RING, PACK, HT), half),
            pltpu.VMEM((RING, PACK, HT), half),
            pltpu.VMEM((2 * RING, DV, DV), half),
            pltpu.VMEM((2, 2, DV, TILE), half),
            pltpu.VMEM((DV, TILE), half),
            pltpu.VMEM((2, DV, DV), jnp.float32),
            pltpu.VMEM((CHUNKS, ROWS, DV), half),
            pltpu.VMEM((CHUNKS, ROWS, DV), half),
            pltpu.VMEM((CHUNKS, ROWS, DV), half),
            pltpu.VMEM((CHUNKS, ROWS, DV), half),
            dma((RING,)), dma((RING,)), dma((2,)), dma((RING,)), dma((2, 2)), dma((2, 2)),
            dma((CHUNKS,)), dma((CHUNKS,)), dma((CHUNKS,)), dma((CHUNKS,)),
        ],
        compiler_params=pltpu.CompilerParams(
            collective_id=0, has_side_effects=True, vmem_limit_bytes=36 << 20
        ),
        name="ladder",
    )(pack, weighted)
    return ladder.reshape(1, 1, DV, DV)


def solution(mesh):
    return jax.shard_map(
        shards,
        mesh=mesh,
        in_specs=(
            P("orow", "ocol", None, None),
            P("orow", "ocol", None, None),
            P(),
            P("ocol", None, None),
        ),
        out_specs=P("orow", "ocol", None, None),
        check_vma=False,
    )
```

```python
import jax
import jax.numpy as jnp
from jax import lax
from jax.experimental import pallas as pl
from jax.experimental.pallas import tpu as pltpu
from jax.sharding import PartitionSpec as P

TILE = 256
HT = 128
DV = 512
NO = 16
RING = 8
CHUNKS = 4
SENDS = 8
LATE = 5
ROWS = DV // CHUNKS
PART = DV // SENDS
PACK = 8 * HT + 16
MESH = pl.DeviceIdType.MESH


def flip(index):
    return index + RING - 2 * RING * (index // RING)


def gives(i, j):
    even = (i // 4 + j // 4 + i + j) % 2 == 0
    return jnp.logical_or(jnp.logical_and(i > j, jnp.logical_not(even)), jnp.logical_and(i < j, even))


def corner(shape=(HT, HT)):
    return lax.broadcasted_iota(jnp.int32, shape, 0), lax.broadcasted_iota(jnp.int32, shape, 1)


def prep_kernel(tiles_ref, mask_ref, amp_ref, chol_ref, pack_ref, weighted_ref, stage, raw, sems, raw_sem):
    i = lax.axis_index("orow")
    half = lax.axis_index("ocol") // RING
    raw_copy = pltpu.make_async_copy(amp_ref, raw, raw_sem)
    copies = []
    for s in range(RING + 1):
        if s < RING:
            j = half * RING + s
            other = jnp.logical_and(i // RING == half, gives(i, j))
            a = jnp.where(other, flip(i), i)
            b = jnp.where(other, flip(j), j)
        else:
            a = b = flip(i)
        t0 = tiles_ref[a, 0, b] * TILE
        t1 = tiles_ref[a, 1, b] * TILE

        def pick(row, col, height, dst, sem):
            copy = pltpu.make_async_copy(
                chol_ref.at[0, pl.ds(pl.multiple_of(row, HT), height), pl.ds(pl.multiple_of(col, HT), HT)], dst, sem
            )
            copy.start()
            return copy

        mine = []
        for n, (t, off) in enumerate(((t0, 0), (t0, HT), (t1, 0), (t1, HT))):
            mine.append(pick(t + off, t + off, HT, stage.at[s, n], sems.at[s, n]))
        for n, (row, col, height, at) in enumerate(
            ((t0, t1, TILE, 0), (t0, t1 + HT, TILE, TILE), (t0, t0 + HT, HT, 2 * TILE), (t1, t1 + HT, HT, 2 * TILE + HT))
        ):
            mine.append(pick(row, col, height, pack_ref.at[s, pl.ds(at, height)], sems.at[s, 4 + n]))
        copies.append(mine)
        if s == 0:
            raw_copy.start()
    row, col = corner()
    line = lax.broadcasted_iota(jnp.int32, (16, HT), 0)
    raw_copy.wait()
    for s in range(2):
        for t in range(2):
            keep = mask_ref[0, 0, s, t].astype(jnp.float32).astype(jnp.bfloat16)
            weighted_ref[t, pl.ds(s * TILE, TILE), :] = raw[0, 0, pl.ds(s * TILE, TILE), pl.ds(t * TILE, TILE)] * keep
    for s in range(RING + 1):
        for n in range(4):
            copies[s][n].wait()
        blocks = [stage[s, n].astype(jnp.float32) for n in range(4)]
        pack_ref[s, 6 * HT : 7 * HT, :] = jnp.where(row <= col, blocks[0], blocks[1]).astype(jnp.bfloat16)
        pack_ref[s, 7 * HT : 8 * HT, :] = jnp.where(row <= col, blocks[2], blocks[3]).astype(jnp.bfloat16)
        ends = [jnp.sum(jnp.where(row == col, blocks[n], 0.0), axis=0, keepdims=True) for n in (1, 3)]
        pack_ref[s, 8 * HT :, :] = jnp.where(line == 0, ends[0], ends[1]).astype(jnp.bfloat16)
    for s in range(RING + 1):
        for n in range(4, 8):
            copies[s][n].wait()


def ladder_kernel(
    pack_ref, weighted_ref, out_ref,
    slots, extra, factor, inputs, inner, total, give, got, pass_on, passed,
    f_send, f_recv, x_send, x_recv, w_send, w_recv, p_send, p_recv, m_send, m_recv,
):
    i = lax.axis_index("orow")
    j = lax.axis_index("ocol")
    half = j // RING
    me = j - half * RING
    y, core = me // 2, me % 2
    fi, fj = flip(i), flip(j)
    same = i // RING == half
    diag = i == j
    lower = jnp.logical_and(same, gives(i, j))
    upper = jnp.logical_and(same, gives(j, i))
    not_lower = jnp.logical_not(lower)
    not_upper = jnp.logical_not(upper)
    swapped = jnp.logical_or(upper, diag)
    dflag = jnp.where(diag, 1, 0)
    w_dev = (jnp.where(swapped, fj, j), jnp.where(swapped, fi, i))
    p_swap = jnp.logical_or(lower, diag)
    p_dev = (jnp.where(p_swap, fj, j), jnp.where(p_swap, fi, i))
    m_dev = (fi, fj)
    t_dev = (j, i)

    def peer(k):
        step = k // 2
        dy = step + step // 2 - 2 * (step // 3)
        return ((y + dy) % 4) * 2 + (core + k) % 2

    barrier = pltpu.get_barrier_semaphore()

    def greet(device):
        pl.semaphore_signal(barrier, inc=1, device_id=device, device_id_type=MESH)

    for k in range(1, RING):
        greet((i, half * RING + peer(k)))
    greet(w_dev)

    @pl.when(jnp.logical_or(upper, lower))
    def _():
        greet(p_dev)

    @pl.when(lower)
    def _():
        greet(m_dev)

    pl.semaphore_wait(barrier, RING + jnp.where(diag, 0, jnp.where(same, 1, 0)) + jnp.where(lower, 1, 0))

    def remote(src, dst, send, recv, device):
        return pltpu.make_async_remote_copy(
            src_ref=src, dst_ref=dst, send_sem=send, recv_sem=recv, device_id=device, device_id_type=MESH
        )

    def w_copy(h):
        return remote(weighted_ref.at[h], inputs.at[1, h], w_send.at[1, h], w_recv.at[1, h], w_dev)

    def w_more(h):
        return remote(weighted_ref.at[h], inputs.at[0, h], w_send.at[0, h], w_recv.at[0, h], m_dev)

    def w_own(h):
        return pltpu.make_async_copy(weighted_ref.at[h], inputs.at[0, h], w_recv.at[0, h])

    for h in range(2):
        w_copy(h).start()

        @pl.when(lower)
        def _():
            w_more(h).start()

        @pl.when(not_lower)
        def _():
            w_own(h).start()

    def f_copy(k):
        to = peer(k)
        return remote(pack_ref.at[to], slots.at[me], f_send.at[k], f_recv.at[me], (i, half * RING + to))

    f_own = pltpu.make_async_copy(pack_ref.at[me], slots.at[me], f_send.at[0])
    f_own.start()
    x_copy = remote(pack_ref.at[RING], extra.at[me], x_send.at[0], x_recv.at[me], (i, i))
    x_own = pltpu.make_async_copy(pack_ref.at[RING], extra.at[me], x_send.at[1])
    for k in range(1, RING):
        f_copy(k).start()

    @pl.when(jnp.logical_and(same, jnp.logical_not(diag)))
    def _():
        x_copy.start()

    @pl.when(diag)
    def _():
        x_own.start()

    total[...] = jnp.zeros_like(total)

    @pl.when(not_lower)
    def _():
        for h in range(2):
            w_own(h).wait()

    f_own.wait()

    @pl.when(diag)
    def _():
        x_own.wait()

    row, col = corner()

    def build(source, slot, which):
        for n in range(2):
            at = n * TILE
            side = source[slot, 4 * HT + n * HT : 5 * HT + n * HT, :]
            mixed = source[slot, 6 * HT + n * HT : 7 * HT + n * HT, :].astype(jnp.float32)
            turned = mixed.T
            ends = source[slot, 8 * HT :, :].astype(jnp.float32)[n : n + 1, :]
            factor[which, at : at + HT, at : at + HT] = jnp.where(row <= col, mixed, turned).astype(jnp.bfloat16)
            factor[which, at : at + HT, at + HT : at + TILE] = side
            factor[which, at + HT : at + TILE, at : at + HT] = side.T
            factor[which, at + HT : at + TILE, at + HT : at + TILE] = jnp.where(
                row > col, mixed, jnp.where(row == col, ends, turned)
            ).astype(jnp.bfloat16)
            block = source[slot, n * TILE : n * TILE + TILE, :]
            factor[which, :TILE, TILE + n * HT : TILE + n * HT + HT] = block
            factor[which, TILE + n * HT : TILE + n * HT + HT, :TILE] = block.T

    def add(side, which):
        for h in range(2):
            inner[:, h * TILE : h * TILE + TILE] = jnp.dot(
                factor[which], inputs[side, h], preferred_element_type=jnp.float32
            ).astype(jnp.bfloat16)
        for c in range(2):
            cols = pl.ds(c * TILE, TILE)
            total[side, :, cols] += jnp.dot(
                inner[...], factor[which, :, cols], preferred_element_type=jnp.float32
            )

    def await_inputs():
        for h in range(2):
            w_copy(h).wait_recv()

        @pl.when(lower)
        def _():
            for h in range(2):
                w_more(h).wait_recv()

    def step(k, carry):
        slot = peer(k)

        @pl.when(k > 0)
        def _():
            remote(pack_ref.at[slot], slots.at[slot], f_send.at[slot], f_recv.at[slot], w_dev).wait_recv()

        build(slots, slot, k)

        @pl.when(diag)
        def _():
            @pl.when(k > 0)
            def _():
                remote(pack_ref.at[RING], extra.at[slot], x_send.at[0], x_recv.at[slot], w_dev).wait_recv()

            build(extra, slot, k + RING)

        @pl.when(not_lower)
        def _():
            add(0, k)

        @pl.when(k == LATE)
        def _():
            await_inputs()

        def again(n, carry):
            add(1, n + RING * dflag)

            @pl.when(lower)
            def _():
                add(0, n)

            return carry

        lax.fori_loop(jnp.where(k == LATE, 0, k), jnp.where(k < LATE, 0, k + 1), again, 0)
        return carry

    lax.fori_loop(0, RING, step, 0)

    def p_copy(r):
        return remote(give.at[r], got.at[r], p_send.at[r], p_recv.at[r], p_dev)

    def m_copy(r):
        return remote(pass_on.at[r], passed.at[r], m_send.at[r], m_recv.at[r], t_dev)

    @pl.when(not_upper)
    def _():
        for r in range(CHUNKS):
            rows = pl.ds(r * ROWS, ROWS)
            ours = (total[1, rows, :] + total[dflag, :, rows].T).astype(jnp.bfloat16)
            for n in range(2):
                give[2 * r + n] = ours[n * PART : (n + 1) * PART]
                p_copy(2 * r + n).start()

    @pl.when(not_lower)
    def _():
        for r in range(CHUNKS):
            rows = pl.ds(r * ROWS, ROWS)
            out_ref[rows, :] = total[0, rows, :] + total[1 - dflag, :, rows].T
        for r in range(SENDS):
            rows = pl.ds(r * PART, PART)
            p_copy(r).wait_recv()
            ours = out_ref[rows, :] + got[r].astype(jnp.float32)
            out_ref[rows, :] = ours

            @pl.when(upper)
            def _():
                pass_on[r] = ours.astype(jnp.bfloat16)
                m_copy(r).start()

    @pl.when(lower)
    def _():
        for r in range(CHUNKS):
            for n in range(2):
                m_copy(2 * r + n).wait_recv()
            both = jnp.concatenate([passed[2 * r], passed[2 * r + 1]], axis=0)
            out_ref[:, pl.ds(r * ROWS, ROWS)] = both.astype(jnp.float32).T

    for h in range(2):
        w_copy(h).wait_send()
    for k in range(1, RING):
        f_copy(k).wait_send()

    @pl.when(not_upper)
    def _():
        for r in range(SENDS):
            p_copy(r).wait_send()

    @pl.when(upper)
    def _():
        for r in range(SENDS):
            m_copy(r).wait_send()

    @pl.when(jnp.logical_and(same, jnp.logical_not(diag)))
    def _():
        x_copy.wait_send()

    @pl.when(lower)
    def _():
        for h in range(2):
            w_more(h).wait_send()


def shards(amplitudes, tile_mask, domain_tiles, cholesky):
    vmem = pl.BlockSpec(memory_space=pltpu.VMEM)
    smem = pl.BlockSpec(memory_space=pltpu.SMEM)
    hbm = pl.BlockSpec(memory_space=pl.ANY)
    dma = pltpu.SemaphoreType.DMA
    half = jnp.bfloat16
    pack, weighted = pl.pallas_call(
        prep_kernel,
        out_shape=(
            pltpu.VMEM((RING + 1, PACK, HT), half),
            pltpu.VMEM((2, DV, TILE), half),
        ),
        in_specs=[smem, smem, hbm, hbm],
        out_specs=(vmem, vmem),
        scratch_shapes=[
            pltpu.VMEM((RING + 1, 4, HT, HT), half),
            pltpu.VMEM((1, 1, DV, DV), half),
            dma((RING + 1, 8)),
            dma,
        ],
        compiler_params=pltpu.CompilerParams(vmem_limit_bytes=56 << 20),
        name="prep",
    )(domain_tiles.transpose(0, 2, 1), tile_mask, amplitudes, cholesky)
    ladder = pl.pallas_call(
        ladder_kernel,
        out_shape=jax.ShapeDtypeStruct((DV, DV), jnp.float32),
        in_specs=[vmem, vmem],
        out_specs=vmem,
        scratch_shapes=[
            pltpu.VMEM((RING, PACK, HT), half),
            pltpu.VMEM((RING, PACK, HT), half),
            pltpu.VMEM((2 * RING, DV, DV), half),
            pltpu.VMEM((2, 2, DV, TILE), half),
            pltpu.VMEM((DV, DV), half),
            pltpu.VMEM((2, DV, DV), jnp.float32),
            pltpu.VMEM((SENDS, PART, DV), half),
            pltpu.VMEM((SENDS, PART, DV), half),
            pltpu.VMEM((SENDS, PART, DV), half),
            pltpu.VMEM((SENDS, PART, DV), half),
            dma((RING,)), dma((RING,)), dma((2,)), dma((RING,)), dma((2, 2)), dma((2, 2)),
            dma((SENDS,)), dma((SENDS,)), dma((SENDS,)), dma((SENDS,)),
        ],
        compiler_params=pltpu.CompilerParams(
            collective_id=0, has_side_effects=True, vmem_limit_bytes=36 << 20
        ),
        name="ladder",
    )(pack, weighted)
    return ladder.reshape(1, 1, DV, DV)


def solution(mesh):
    return jax.shard_map(
        shards,
        mesh=mesh,
        in_specs=(
            P("orow", "ocol", None, None),
            P("orow", "ocol", None, None),
            P(),
            P("ocol", None, None),
        ),
        out_specs=P("orow", "ocol", None, None),
        check_vma=False,
    )
```

```python
import jax
import jax.numpy as jnp
from jax import lax
from jax.experimental import pallas as pl
from jax.experimental.pallas import tpu as pltpu
from jax.sharding import PartitionSpec as P

TILE = 256
HT = 128
DV = 512
NO = 16
RING = 8
CHUNKS = 4
SENDS = 8
LATE = 5
ROWS = DV // CHUNKS
PART = DV // SENDS
PACK = 8 * HT + 16
MESH = pl.DeviceIdType.MESH


def flip(index):
    return index + RING - 2 * RING * (index // RING)


def gives(i, j):
    even = (i // 4 + j // 4 + i + j) % 2 == 0
    return jnp.logical_or(jnp.logical_and(i > j, jnp.logical_not(even)), jnp.logical_and(i < j, even))


def corner(shape=(HT, HT)):
    return lax.broadcasted_iota(jnp.int32, shape, 0), lax.broadcasted_iota(jnp.int32, shape, 1)


def prep_kernel(tiles_ref, mask_ref, amp_ref, chol_ref, pack_ref, weighted_ref, stage, raw, sems, raw_sem):
    i = lax.axis_index("orow")
    half = lax.axis_index("ocol") // RING
    raw_copy = pltpu.make_async_copy(amp_ref, raw, raw_sem)
    copies = []
    for s in range(RING + 1):
        if s < RING:
            j = half * RING + s
            other = jnp.logical_and(i // RING == half, gives(i, j))
            a = jnp.where(other, flip(i), i)
            b = jnp.where(other, flip(j), j)
        else:
            a = b = flip(i)
        t0 = tiles_ref[a, 0, b] * TILE
        t1 = tiles_ref[a, 1, b] * TILE

        def pick(row, col, height, dst, sem):
            copy = pltpu.make_async_copy(
                chol_ref.at[0, pl.ds(pl.multiple_of(row, HT), height), pl.ds(pl.multiple_of(col, HT), HT)], dst, sem
            )
            copy.start()
            return copy

        mine = []
        for n, (t, off) in enumerate(((t0, 0), (t0, HT), (t1, 0), (t1, HT))):
            mine.append(pick(t + off, t + off, HT, stage.at[s, n], sems.at[s, n]))
        for n, (row, col, height, at) in enumerate(
            ((t0, t1, TILE, 0), (t0, t1 + HT, TILE, TILE), (t0, t0 + HT, HT, 2 * TILE), (t1, t1 + HT, HT, 2 * TILE + HT))
        ):
            mine.append(pick(row, col, height, pack_ref.at[s, pl.ds(at, height)], sems.at[s, 4 + n]))
        copies.append(mine)
        if s == 0:
            raw_copy.start()
    row, col = corner()
    line = lax.broadcasted_iota(jnp.int32, (16, HT), 0)
    raw_copy.wait()
    for s in range(2):
        for t in range(2):
            keep = mask_ref[0, 0, s, t].astype(jnp.float32).astype(jnp.bfloat16)
            weighted_ref[t, pl.ds(s * TILE, TILE), :] = raw[0, 0, pl.ds(s * TILE, TILE), pl.ds(t * TILE, TILE)] * keep
    for s in range(RING + 1):
        for n in range(4):
            copies[s][n].wait()
        blocks = [stage[s, n].astype(jnp.float32) for n in range(4)]
        pack_ref[s, 6 * HT : 7 * HT, :] = jnp.where(row <= col, blocks[0], blocks[1]).astype(jnp.bfloat16)
        pack_ref[s, 7 * HT : 8 * HT, :] = jnp.where(row <= col, blocks[2], blocks[3]).astype(jnp.bfloat16)
        ends = [jnp.sum(jnp.where(row == col, blocks[n], 0.0), axis=0, keepdims=True) for n in (1, 3)]
        pack_ref[s, 8 * HT :, :] = jnp.where(line == 0, ends[0], ends[1]).astype(jnp.bfloat16)
    for s in range(RING + 1):
        for n in range(4, 8):
            copies[s][n].wait()


def ladder_kernel(
    pack_ref, weighted_ref, out_ref,
    slots, extra, through, factor, inputs, inner, total, give, got, pass_on, passed,
    f_send, f_recv, x_send, x_recv, r_send, r_recv, w_send, w_recv, p_send, p_recv, m_send, m_recv,
):
    i = lax.axis_index("orow")
    j = lax.axis_index("ocol")
    half = j // RING
    me = j - half * RING
    y, core = me // 2, me % 2
    fi, fj = flip(i), flip(j)
    same = i // RING == half
    diag = i == j
    lower = jnp.logical_and(same, gives(i, j))
    upper = jnp.logical_and(same, gives(j, i))
    not_lower = jnp.logical_not(lower)
    not_upper = jnp.logical_not(upper)
    swapped = jnp.logical_or(upper, diag)
    dflag = jnp.where(diag, 1, 0)
    w_dev = (jnp.where(swapped, fj, j), jnp.where(swapped, fi, i))
    p_swap = jnp.logical_or(lower, diag)
    p_dev = (jnp.where(p_swap, fj, j), jnp.where(p_swap, fi, i))
    m_dev = (fi, fj)
    t_dev = (j, i)

    def peer(k):
        step = k // 2
        dy = step + step // 2 - 2 * (step // 3)
        return ((y + dy) % 4) * 2 + (core + k) % 2

    entry = (i // 2) % 4
    ahead = entry % 2 == 0
    place = (y - entry + 4) % 4
    detours = jnp.logical_or(place == 0, place == jnp.where(ahead, 1, 3))
    relays = jnp.logical_not(detours)
    via = (y + jnp.where(jnp.logical_xor(place == 0, ahead), 1, 3)) % 4
    origin = (y + jnp.where(jnp.logical_xor(place == 2, ahead), 1, 3)) % 4

    barrier = pltpu.get_barrier_semaphore()

    def greet(device):
        pl.semaphore_signal(barrier, inc=1, device_id=device, device_id_type=MESH)

    for k in range(1, RING):
        greet((i, half * RING + peer(k)))
    greet(w_dev)

    @pl.when(jnp.logical_or(upper, lower))
    def _():
        greet(p_dev)

    @pl.when(lower)
    def _():
        greet(m_dev)

    pl.semaphore_wait(barrier, RING + jnp.where(diag, 0, jnp.where(same, 1, 0)) + jnp.where(lower, 1, 0))

    def remote(src, dst, send, recv, device):
        return pltpu.make_async_remote_copy(
            src_ref=src, dst_ref=dst, send_sem=send, recv_sem=recv, device_id=device, device_id_type=MESH
        )

    def w_copy(h):
        return remote(weighted_ref.at[h], inputs.at[1, h], w_send.at[1, h], w_recv.at[1, h], w_dev)

    def w_more(h):
        return remote(weighted_ref.at[h], inputs.at[0, h], w_send.at[0, h], w_recv.at[0, h], m_dev)

    def w_own(h):
        return pltpu.make_async_copy(weighted_ref.at[h], inputs.at[0, h], w_recv.at[0, h])

    for h in range(2):
        w_copy(h).start()

        @pl.when(lower)
        def _():
            w_more(h).start()

        @pl.when(not_lower)
        def _():
            w_own(h).start()

    def f_copy(k):
        to = peer(k)
        return remote(pack_ref.at[to], slots.at[me], f_send.at[k], f_recv.at[me], (i, half * RING + to))

    def detour(n):
        to = peer(RING - 2 + n)
        return remote(
            pack_ref.at[to], through.at[n], f_send.at[RING - 2 + n], r_recv.at[n], (i, half * RING + via * 2 + core)
        )

    def forward(n):
        at = origin * 2 + core
        to = half * RING + (origin + 2) % 4 * 2 + (core + n) % 2
        return remote(through.at[n], slots.at[at], r_send.at[n], f_recv.at[at], (i, to))

    f_own = pltpu.make_async_copy(pack_ref.at[me], slots.at[me], f_send.at[0])
    f_own.start()
    x_copy = remote(pack_ref.at[RING], extra.at[me], x_send.at[0], x_recv.at[me], (i, i))
    x_own = pltpu.make_async_copy(pack_ref.at[RING], extra.at[me], x_send.at[1])
    @pl.when(detours)
    def _():
        for n in range(2):
            detour(n).start()

    for k in range(1, RING - 2):
        f_copy(k).start()

    @pl.when(relays)
    def _():
        for k in range(RING - 2, RING):
            f_copy(k).start()

    @pl.when(jnp.logical_and(same, jnp.logical_not(diag)))
    def _():
        x_copy.start()

    @pl.when(diag)
    def _():
        x_own.start()

    total[...] = jnp.zeros_like(total)

    @pl.when(not_lower)
    def _():
        for h in range(2):
            w_own(h).wait()

    f_own.wait()

    @pl.when(diag)
    def _():
        x_own.wait()

    row, col = corner()

    def build(source, slot, which):
        for n in range(2):
            at = n * TILE
            side = source[slot, 4 * HT + n * HT : 5 * HT + n * HT, :]
            mixed = source[slot, 6 * HT + n * HT : 7 * HT + n * HT, :].astype(jnp.float32)
            turned = mixed.T
            ends = source[slot, 8 * HT :, :].astype(jnp.float32)[n : n + 1, :]
            factor[which, at : at + HT, at : at + HT] = jnp.where(row <= col, mixed, turned).astype(jnp.bfloat16)
            factor[which, at : at + HT, at + HT : at + TILE] = side
            factor[which, at + HT : at + TILE, at : at + HT] = side.T
            factor[which, at + HT : at + TILE, at + HT : at + TILE] = jnp.where(
                row > col, mixed, jnp.where(row == col, ends, turned)
            ).astype(jnp.bfloat16)
            block = source[slot, n * TILE : n * TILE + TILE, :]
            factor[which, :TILE, TILE + n * HT : TILE + n * HT + HT] = block
            factor[which, TILE + n * HT : TILE + n * HT + HT, :TILE] = block.T

    def add(side, which):
        for h in range(2):
            inner[:, h * TILE : h * TILE + TILE] = jnp.dot(
                factor[which], inputs[side, h], preferred_element_type=jnp.float32
            ).astype(jnp.bfloat16)
        for c in range(2):
            cols = pl.ds(c * TILE, TILE)
            total[side, :, cols] += jnp.dot(
                inner[...], factor[which, :, cols], preferred_element_type=jnp.float32
            )

    def await_inputs():
        for h in range(2):
            w_copy(h).wait_recv()

        @pl.when(lower)
        def _():
            for h in range(2):
                w_more(h).wait_recv()

    def again(n, carry):
        add(1, n + RING * dflag)

        @pl.when(lower)
        def _():
            add(0, n)

        return carry

    def step(k, carry):
        slot = peer(k)

        @pl.when(k == LATE)
        def _():
            await_inputs()
            lax.fori_loop(0, LATE, again, 0)

        @pl.when(jnp.logical_and(relays, k == 1))
        def _():
            for n in range(2):
                detour(n).wait_recv()
                forward(n).start()

        @pl.when(k > 0)
        def _():
            remote(pack_ref.at[slot], slots.at[slot], f_send.at[slot], f_recv.at[slot], w_dev).wait_recv()

        build(slots, slot, k)

        @pl.when(diag)
        def _():
            @pl.when(k > 0)
            def _():
                remote(pack_ref.at[RING], extra.at[slot], x_send.at[0], x_recv.at[slot], w_dev).wait_recv()

            build(extra, slot, k + RING)

        @pl.when(not_lower)
        def _():
            add(0, k)

        lax.fori_loop(k, jnp.where(k < LATE, k, k + 1), again, 0)
        return carry

    lax.fori_loop(0, RING, step, 0)

    def p_copy(r):
        return remote(give.at[r], got.at[r], p_send.at[r], p_recv.at[r], p_dev)

    def m_copy(r):
        return remote(pass_on.at[r], passed.at[r], m_send.at[r], m_recv.at[r], t_dev)

    @pl.when(not_upper)
    def _():
        for r in range(CHUNKS):
            rows = pl.ds(r * ROWS, ROWS)
            ours = (total[1, rows, :] + total[dflag, :, rows].T).astype(jnp.bfloat16)
            for n in range(2):
                give[2 * r + n] = ours[n * PART : (n + 1) * PART]
                p_copy(2 * r + n).start()

    @pl.when(not_lower)
    def _():
        for r in range(CHUNKS):
            rows = pl.ds(r * ROWS, ROWS)
            out_ref[rows, :] = total[0, rows, :] + total[1 - dflag, :, rows].T
        for r in range(SENDS):
            rows = pl.ds(r * PART, PART)
            p_copy(r).wait_recv()
            ours = out_ref[rows, :] + got[r].astype(jnp.float32)
            out_ref[rows, :] = ours

            @pl.when(upper)
            def _():
                pass_on[r] = ours.astype(jnp.bfloat16)
                m_copy(r).start()

    @pl.when(lower)
    def _():
        for r in range(CHUNKS):
            for n in range(2):
                m_copy(2 * r + n).wait_recv()
            both = jnp.concatenate([passed[2 * r], passed[2 * r + 1]], axis=0)
            out_ref[:, pl.ds(r * ROWS, ROWS)] = both.astype(jnp.float32).T

    for h in range(2):
        w_copy(h).wait_send()
    for k in range(1, RING):
        f_copy(k).wait_send()

    @pl.when(relays)
    def _():
        for n in range(2):
            forward(n).wait_send()

    @pl.when(not_upper)
    def _():
        for r in range(SENDS):
            p_copy(r).wait_send()

    @pl.when(upper)
    def _():
        for r in range(SENDS):
            m_copy(r).wait_send()

    @pl.when(jnp.logical_and(same, jnp.logical_not(diag)))
    def _():
        x_copy.wait_send()

    @pl.when(lower)
    def _():
        for h in range(2):
            w_more(h).wait_send()


def shards(amplitudes, tile_mask, domain_tiles, cholesky):
    vmem = pl.BlockSpec(memory_space=pltpu.VMEM)
    smem = pl.BlockSpec(memory_space=pltpu.SMEM)
    hbm = pl.BlockSpec(memory_space=pl.ANY)
    dma = pltpu.SemaphoreType.DMA
    half = jnp.bfloat16
    pack, weighted = pl.pallas_call(
        prep_kernel,
        out_shape=(
            pltpu.VMEM((RING + 1, PACK, HT), half),
            pltpu.VMEM((2, DV, TILE), half),
        ),
        in_specs=[smem, smem, hbm, hbm],
        out_specs=(vmem, vmem),
        scratch_shapes=[
            pltpu.VMEM((RING + 1, 4, HT, HT), half),
            pltpu.VMEM((1, 1, DV, DV), half),
            dma((RING + 1, 8)),
            dma,
        ],
        compiler_params=pltpu.CompilerParams(vmem_limit_bytes=56 << 20),
        name="prep",
    )(domain_tiles.transpose(0, 2, 1), tile_mask, amplitudes, cholesky)
    ladder = pl.pallas_call(
        ladder_kernel,
        out_shape=jax.ShapeDtypeStruct((DV, DV), jnp.float32),
        in_specs=[vmem, vmem],
        out_specs=vmem,
        scratch_shapes=[
            pltpu.VMEM((RING, PACK, HT), half),
            pltpu.VMEM((RING, PACK, HT), half),
            pltpu.VMEM((2, PACK, HT), half),
            pltpu.VMEM((2 * RING, DV, DV), half),
            pltpu.VMEM((2, 2, DV, TILE), half),
            pltpu.VMEM((DV, DV), half),
            pltpu.VMEM((2, DV, DV), jnp.float32),
            pltpu.VMEM((SENDS, PART, DV), half),
            pltpu.VMEM((SENDS, PART, DV), half),
            pltpu.VMEM((SENDS, PART, DV), half),
            pltpu.VMEM((SENDS, PART, DV), half),
            dma((RING,)), dma((RING,)), dma((2,)), dma((RING,)), dma((2,)), dma((2,)), dma((2, 2)), dma((2, 2)),
            dma((SENDS,)), dma((SENDS,)), dma((SENDS,)), dma((SENDS,)),
        ],
        compiler_params=pltpu.CompilerParams(
            collective_id=0, has_side_effects=True, vmem_limit_bytes=36 << 20
        ),
        name="ladder",
    )(pack, weighted)
    return ladder.reshape(1, 1, DV, DV)


def solution(mesh):
    return jax.shard_map(
        shards,
        mesh=mesh,
        in_specs=(
            P("orow", "ocol", None, None),
            P("orow", "ocol", None, None),
            P(),
            P("ocol", None, None),
        ),
        out_specs=P("orow", "ocol", None, None),
        check_vma=False,
    )
```

```python
import jax
import jax.numpy as jnp
from jax import lax
from jax.experimental import pallas as pl
from jax.experimental.pallas import tpu as pltpu
from jax.sharding import PartitionSpec as P

TILE = 256
HT = 128
DV = 512
NO = 16
RING = 8
CHUNKS = 4
SENDS = 8
REST = 4
LATE = 5
ROWS = DV // CHUNKS
PART = DV // SENDS
PACK = 8 * HT + 16
MESH = pl.DeviceIdType.MESH


def flip(index):
    return index + RING - 2 * RING * (index // RING)


def gives(i, j):
    even = (i // 4 + j // 4 + i + j) % 2 == 0
    return jnp.logical_or(jnp.logical_and(i > j, jnp.logical_not(even)), jnp.logical_and(i < j, even))


def leads(i, j):
    near = i // RING == j // RING
    return jnp.logical_or(
        jnp.logical_and(near, gives(i, j)), jnp.logical_and(jnp.logical_not(near), (i + j) % 2 == 0)
    )


def corner(shape=(HT, HT)):
    return lax.broadcasted_iota(jnp.int32, shape, 0), lax.broadcasted_iota(jnp.int32, shape, 1)


def prep_kernel(tiles_ref, mask_ref, amp_ref, chol_ref, pack_ref, weighted_ref, stage, raw, sems, raw_sem):
    i = lax.axis_index("orow")
    half = lax.axis_index("ocol") // RING
    raw_copy = pltpu.make_async_copy(amp_ref, raw, raw_sem)
    copies = []
    for s in range(RING + 1):
        if s < RING:
            j = half * RING + s
            other = jnp.logical_and(i // RING == half, gives(i, j))
            a = jnp.where(other, flip(i), i)
            b = jnp.where(other, flip(j), j)
        else:
            a = b = flip(i)
        t0 = tiles_ref[a, 0, b] * TILE
        t1 = tiles_ref[a, 1, b] * TILE

        def pick(row, col, height, dst, sem):
            copy = pltpu.make_async_copy(
                chol_ref.at[0, pl.ds(pl.multiple_of(row, HT), height), pl.ds(pl.multiple_of(col, HT), HT)], dst, sem
            )
            copy.start()
            return copy

        mine = []
        for n, (t, off) in enumerate(((t0, 0), (t0, HT), (t1, 0), (t1, HT))):
            mine.append(pick(t + off, t + off, HT, stage.at[s, n], sems.at[s, n]))
        for n, (row, col, height, at) in enumerate(
            ((t0, t1, TILE, 0), (t0, t1 + HT, TILE, TILE), (t0, t0 + HT, HT, 2 * TILE), (t1, t1 + HT, HT, 2 * TILE + HT))
        ):
            mine.append(pick(row, col, height, pack_ref.at[s, pl.ds(at, height)], sems.at[s, 4 + n]))
        copies.append(mine)
        if s == 0:
            raw_copy.start()
    row, col = corner()
    line = lax.broadcasted_iota(jnp.int32, (16, HT), 0)
    raw_copy.wait()
    for s in range(2):
        for t in range(2):
            keep = mask_ref[0, 0, s, t].astype(jnp.float32).astype(jnp.bfloat16)
            weighted_ref[t, pl.ds(s * TILE, TILE), :] = raw[0, 0, pl.ds(s * TILE, TILE), pl.ds(t * TILE, TILE)] * keep
    for s in range(RING + 1):
        for n in range(4):
            copies[s][n].wait()
        blocks = [stage[s, n].astype(jnp.float32) for n in range(4)]
        pack_ref[s, 6 * HT : 7 * HT, :] = jnp.where(row <= col, blocks[0], blocks[1]).astype(jnp.bfloat16)
        pack_ref[s, 7 * HT : 8 * HT, :] = jnp.where(row <= col, blocks[2], blocks[3]).astype(jnp.bfloat16)
        ends = [jnp.sum(jnp.where(row == col, blocks[n], 0.0), axis=0, keepdims=True) for n in (1, 3)]
        pack_ref[s, 8 * HT :, :] = jnp.where(line == 0, ends[0], ends[1]).astype(jnp.bfloat16)
    for s in range(RING + 1):
        for n in range(4, 8):
            copies[s][n].wait()


def ladder_kernel(
    pack_ref, weighted_ref, out_ref,
    slots, extra, through, factor, inputs, inner, total, give, got, pass_on, passed,
    f_send, f_recv, x_send, x_recv, r_send, r_recv, w_send, w_recv, p_send, p_recv, m_send, m_recv,
):
    i = lax.axis_index("orow")
    j = lax.axis_index("ocol")
    half = j // RING
    me = j - half * RING
    y, core = me // 2, me % 2
    fi, fj = flip(i), flip(j)
    same = i // RING == half
    diag = i == j
    lower = jnp.logical_and(same, gives(i, j))
    upper = jnp.logical_and(same, gives(j, i))
    not_lower = jnp.logical_not(lower)
    not_upper = jnp.logical_not(upper)
    swapped = jnp.logical_or(upper, diag)
    dflag = jnp.where(diag, 1, 0)
    w_dev = (jnp.where(swapped, fj, j), jnp.where(swapped, fi, i))
    p_swap = jnp.logical_or(lower, diag)
    p_dev = (jnp.where(p_swap, fj, j), jnp.where(p_swap, fi, i))
    m_dev = (fi, fj)
    t_dev = (j, i)

    def peer(k):
        step = k // 2
        dy = step + step // 2 - 2 * (step // 3)
        return ((y + dy) % 4) * 2 + (core + k) % 2

    entry = (i // 2) % 4
    ahead = entry % 2 == 0
    place = (y - entry + 4) % 4
    detours = jnp.logical_or(place == 0, place == jnp.where(ahead, 1, 3))
    relays = jnp.logical_not(detours)
    via = (y + jnp.where(jnp.logical_xor(place == 0, ahead), 1, 3)) % 4
    origin = (y + jnp.where(jnp.logical_xor(place == 2, ahead), 1, 3)) % 4

    barrier = pltpu.get_barrier_semaphore()

    def greet(device):
        pl.semaphore_signal(barrier, inc=1, device_id=device, device_id_type=MESH)

    for k in range(1, RING):
        greet((i, half * RING + peer(k)))
    greet(w_dev)

    @pl.when(jnp.logical_or(upper, lower))
    def _():
        greet(p_dev)

    @pl.when(lower)
    def _():
        greet(m_dev)

    pl.semaphore_wait(barrier, RING + jnp.where(diag, 0, jnp.where(same, 1, 0)) + jnp.where(lower, 1, 0))

    def remote(src, dst, send, recv, device):
        return pltpu.make_async_remote_copy(
            src_ref=src, dst_ref=dst, send_sem=send, recv_sem=recv, device_id=device, device_id_type=MESH
        )

    def w_copy(h):
        return remote(weighted_ref.at[h], inputs.at[1, h], w_send.at[1, h], w_recv.at[1, h], w_dev)

    def w_more(h):
        return remote(weighted_ref.at[h], inputs.at[0, h], w_send.at[0, h], w_recv.at[0, h], m_dev)

    def w_own(h):
        return pltpu.make_async_copy(weighted_ref.at[h], inputs.at[0, h], w_recv.at[0, h])

    lead = leads(i, j)
    w_first = jnp.logical_or(upper, jnp.logical_and(lead, jnp.logical_not(same)))

    @pl.when(w_first)
    def _():
        for h in range(2):
            w_copy(h).start()

    for h in range(2):

        @pl.when(lower)
        def _():
            w_more(h).start()

        @pl.when(not_lower)
        def _():
            w_own(h).start()

    def leading(k):
        return leads(i, half * RING + peer(k))

    def f_copy(k):
        to = peer(k)
        return remote(pack_ref.at[to], slots.at[me], f_send.at[k], f_recv.at[me], (i, half * RING + to))

    def detour(n):
        to = peer(RING - 2 + n)
        return remote(
            pack_ref.at[to], through.at[n], f_send.at[RING - 2 + n], r_recv.at[n], (i, half * RING + via * 2 + core)
        )

    def forward(n):
        at = origin * 2 + core
        to = half * RING + (origin + 2) % 4 * 2 + (core + n) % 2
        return remote(through.at[n], slots.at[at], r_send.at[n], f_recv.at[at], (i, to))

    f_own = pltpu.make_async_copy(pack_ref.at[me], slots.at[me], f_send.at[0])
    f_own.start()
    x_copy = remote(pack_ref.at[RING], extra.at[me], x_send.at[0], x_recv.at[me], (i, i))
    x_own = pltpu.make_async_copy(pack_ref.at[RING], extra.at[me], x_send.at[1])
    def send_factors(first):
        for n in range(2):

            @pl.when(jnp.logical_and(detours, leading(RING - 2 + n) == first))
            def _():
                detour(n).start()

        for k in range(1, RING):

            @pl.when(jnp.logical_and(leading(k) == first, relays if k >= RING - 2 else True))
            def _():
                f_copy(k).start()

    send_factors(True)
    send_factors(False)

    @pl.when(jnp.logical_and(same, jnp.logical_not(diag)))
    def _():
        x_copy.start()

    @pl.when(diag)
    def _():
        x_own.start()

    total[...] = jnp.zeros_like(total)

    @pl.when(jnp.logical_not(w_first))
    def _():
        for k in range(1, RING):

            @pl.when(leading(k))
            def _():
                f_copy(k).wait_send()

        for h in range(2):
            w_copy(h).start()

    @pl.when(not_lower)
    def _():
        for h in range(2):
            w_own(h).wait()

    f_own.wait()

    @pl.when(diag)
    def _():
        x_own.wait()

    row, col = corner()

    def build(source, slot, which):
        for n in range(2):
            at = n * TILE
            side = source[slot, 4 * HT + n * HT : 5 * HT + n * HT, :]
            mixed = source[slot, 6 * HT + n * HT : 7 * HT + n * HT, :].astype(jnp.float32)
            turned = mixed.T
            ends = source[slot, 8 * HT :, :].astype(jnp.float32)[n : n + 1, :]
            factor[which, at : at + HT, at : at + HT] = jnp.where(row <= col, mixed, turned).astype(jnp.bfloat16)
            factor[which, at : at + HT, at + HT : at + TILE] = side
            factor[which, at + HT : at + TILE, at : at + HT] = side.T
            factor[which, at + HT : at + TILE, at + HT : at + TILE] = jnp.where(
                row > col, mixed, jnp.where(row == col, ends, turned)
            ).astype(jnp.bfloat16)
            block = source[slot, n * TILE : n * TILE + TILE, :]
            factor[which, :TILE, TILE + n * HT : TILE + n * HT + HT] = block
            factor[which, TILE + n * HT : TILE + n * HT + HT, :TILE] = block.T

    def add(side, which):
        for h in range(2):
            inner[:, h * TILE : h * TILE + TILE] = jnp.dot(
                factor[which], inputs[side, h], preferred_element_type=jnp.float32
            ).astype(jnp.bfloat16)
        for c in range(2):
            cols = pl.ds(c * TILE, TILE)
            total[side, :, cols] += jnp.dot(
                inner[...], factor[which, :, cols], preferred_element_type=jnp.float32
            )

    def await_inputs():
        for h in range(2):
            w_copy(h).wait_recv()

        @pl.when(lower)
        def _():
            for h in range(2):
                w_more(h).wait_recv()

    def again(n, carry):
        add(1, n + RING * dflag)

        @pl.when(lower)
        def _():
            add(0, n)

        return carry

    def step(k, carry):
        slot = peer(k)

        @pl.when(k == LATE)
        def _():
            await_inputs()
            lax.fori_loop(0, LATE, again, 0)

        for n in range(2):
            first = leads(i, half * RING + (origin + 2) % 4 * 2 + (core + n) % 2)

            @pl.when(jnp.logical_and(relays, k == jnp.where(first, 1, REST)))
            def _():
                detour(n).wait_recv()
                forward(n).start()

        @pl.when(k > 0)
        def _():
            remote(pack_ref.at[slot], slots.at[slot], f_send.at[slot], f_recv.at[slot], w_dev).wait_recv()

        build(slots, slot, k)

        @pl.when(diag)
        def _():
            @pl.when(k > 0)
            def _():
                remote(pack_ref.at[RING], extra.at[slot], x_send.at[0], x_recv.at[slot], w_dev).wait_recv()

            build(extra, slot, k + RING)

        @pl.when(not_lower)
        def _():
            add(0, k)

        lax.fori_loop(k, jnp.where(k < LATE, k, k + 1), again, 0)
        return carry

    lax.fori_loop(0, RING, step, 0)

    def p_copy(r):
        return remote(give.at[r], got.at[r], p_send.at[r], p_recv.at[r], p_dev)

    def m_copy(r):
        return remote(pass_on.at[r], passed.at[r], m_send.at[r], m_recv.at[r], t_dev)

    @pl.when(not_upper)
    def _():
        for r in range(CHUNKS):
            rows = pl.ds(r * ROWS, ROWS)
            ours = (total[1, rows, :] + total[dflag, :, rows].T).astype(jnp.bfloat16)
            for n in range(2):
                give[2 * r + n] = ours[n * PART : (n + 1) * PART]
                p_copy(2 * r + n).start()

    @pl.when(not_lower)
    def _():
        for r in range(CHUNKS):
            rows = pl.ds(r * ROWS, ROWS)
            out_ref[rows, :] = total[0, rows, :] + total[1 - dflag, :, rows].T
        for r in range(SENDS):
            rows = pl.ds(r * PART, PART)
            p_copy(r).wait_recv()
            ours = out_ref[rows, :] + got[r].astype(jnp.float32)
            out_ref[rows, :] = ours

            @pl.when(upper)
            def _():
                pass_on[r] = ours.astype(jnp.bfloat16)
                m_copy(r).start()

    @pl.when(lower)
    def _():
        for r in range(CHUNKS):
            for n in range(2):
                m_copy(2 * r + n).wait_recv()
            both = jnp.concatenate([passed[2 * r], passed[2 * r + 1]], axis=0)
            out_ref[:, pl.ds(r * ROWS, ROWS)] = both.astype(jnp.float32).T

    for h in range(2):
        w_copy(h).wait_send()
    for k in range(1, RING):

        @pl.when(jnp.logical_or(w_first, jnp.logical_not(leading(k))))
        def _():
            f_copy(k).wait_send()

    @pl.when(relays)
    def _():
        for n in range(2):
            forward(n).wait_send()

    @pl.when(not_upper)
    def _():
        for r in range(SENDS):
            p_copy(r).wait_send()

    @pl.when(upper)
    def _():
        for r in range(SENDS):
            m_copy(r).wait_send()

    @pl.when(jnp.logical_and(same, jnp.logical_not(diag)))
    def _():
        x_copy.wait_send()

    @pl.when(lower)
    def _():
        for h in range(2):
            w_more(h).wait_send()


def shards(amplitudes, tile_mask, domain_tiles, cholesky):
    vmem = pl.BlockSpec(memory_space=pltpu.VMEM)
    smem = pl.BlockSpec(memory_space=pltpu.SMEM)
    hbm = pl.BlockSpec(memory_space=pl.ANY)
    dma = pltpu.SemaphoreType.DMA
    half = jnp.bfloat16
    pack, weighted = pl.pallas_call(
        prep_kernel,
        out_shape=(
            pltpu.VMEM((RING + 1, PACK, HT), half),
            pltpu.VMEM((2, DV, TILE), half),
        ),
        in_specs=[smem, smem, hbm, hbm],
        out_specs=(vmem, vmem),
        scratch_shapes=[
            pltpu.VMEM((RING + 1, 4, HT, HT), half),
            pltpu.VMEM((1, 1, DV, DV), half),
            dma((RING + 1, 8)),
            dma,
        ],
        compiler_params=pltpu.CompilerParams(vmem_limit_bytes=56 << 20),
        name="prep",
    )(domain_tiles.transpose(0, 2, 1), tile_mask, amplitudes, cholesky)
    ladder = pl.pallas_call(
        ladder_kernel,
        out_shape=jax.ShapeDtypeStruct((DV, DV), jnp.float32),
        in_specs=[vmem, vmem],
        out_specs=vmem,
        scratch_shapes=[
            pltpu.VMEM((RING, PACK, HT), half),
            pltpu.VMEM((RING, PACK, HT), half),
            pltpu.VMEM((2, PACK, HT), half),
            pltpu.VMEM((2 * RING, DV, DV), half),
            pltpu.VMEM((2, 2, DV, TILE), half),
            pltpu.VMEM((DV, DV), half),
            pltpu.VMEM((2, DV, DV), jnp.float32),
            pltpu.VMEM((SENDS, PART, DV), half),
            pltpu.VMEM((SENDS, PART, DV), half),
            pltpu.VMEM((SENDS, PART, DV), half),
            pltpu.VMEM((SENDS, PART, DV), half),
            dma((RING,)), dma((RING,)), dma((2,)), dma((RING,)), dma((2,)), dma((2,)), dma((2, 2)), dma((2, 2)),
            dma((SENDS,)), dma((SENDS,)), dma((SENDS,)), dma((SENDS,)),
        ],
        compiler_params=pltpu.CompilerParams(
            collective_id=0, has_side_effects=True, vmem_limit_bytes=36 << 20
        ),
        name="ladder",
    )(pack, weighted)
    return ladder.reshape(1, 1, DV, DV)


def solution(mesh):
    return jax.shard_map(
        shards,
        mesh=mesh,
        in_specs=(
            P("orow", "ocol", None, None),
            P("orow", "ocol", None, None),
            P(),
            P("ocol", None, None),
        ),
        out_specs=P("orow", "ocol", None, None),
        check_vma=False,
    )
```

```python
import jax
import jax.numpy as jnp
from jax import lax
from jax.experimental import pallas as pl
from jax.experimental.pallas import tpu as pltpu
from jax.sharding import PartitionSpec as P

TILE = 256
HT = 128
DV = 512
NO = 16
RING = 8
CHUNKS = 4
SENDS = 8
REST = 4
SOON = 4
LATE = 5
ROWS = DV // CHUNKS
PART = DV // SENDS
PACK = 8 * HT + 16
MESH = pl.DeviceIdType.MESH


def flip(index):
    return index + RING - 2 * RING * (index // RING)


def gives(i, j):
    even = (i // 4 + j // 4 + i + j) % 2 == 0
    return jnp.logical_or(jnp.logical_and(i > j, jnp.logical_not(even)), jnp.logical_and(i < j, even))


def leads(i, j):
    near = i // RING == j // RING
    return jnp.logical_or(
        jnp.logical_and(near, gives(i, j)), jnp.logical_and(jnp.logical_not(near), (i + j) % 2 == 0)
    )


def corner(shape=(HT, HT)):
    return lax.broadcasted_iota(jnp.int32, shape, 0), lax.broadcasted_iota(jnp.int32, shape, 1)


def prep_kernel(tiles_ref, mask_ref, amp_ref, chol_ref, pack_ref, weighted_ref, stage, raw, sems, raw_sem):
    i = lax.axis_index("orow")
    half = lax.axis_index("ocol") // RING
    raw_copy = pltpu.make_async_copy(amp_ref, raw, raw_sem)
    copies = []
    for s in range(RING + 1):
        if s < RING:
            j = half * RING + s
            other = jnp.logical_and(i // RING == half, gives(i, j))
            a = jnp.where(other, flip(i), i)
            b = jnp.where(other, flip(j), j)
        else:
            a = b = flip(i)
        t0 = tiles_ref[a, 0, b] * TILE
        t1 = tiles_ref[a, 1, b] * TILE

        def pick(row, col, width, dst, sem):
            copy = pltpu.make_async_copy(
                chol_ref.at[0, pl.ds(pl.multiple_of(row, TILE), TILE), pl.ds(pl.multiple_of(col, HT), width)], dst, sem
            )
            copy.start()
            return copy

        mine = [pick(t, t, TILE, stage.at[s, n], sems.at[s, n]) for n, t in enumerate((t0, t1))]
        for n in range(2):
            mine.append(pick(t0, t1 + n * HT, HT, pack_ref.at[s, pl.ds(n * TILE, TILE)], sems.at[s, 2 + n]))
        copies.append(mine)
        if s == 0:
            raw_copy.start()
    row, col = corner()
    line = lax.broadcasted_iota(jnp.int32, (16, HT), 0)
    raw_copy.wait()
    for s in range(2):
        for t in range(2):
            keep = mask_ref[0, 0, s, t].astype(jnp.float32).astype(jnp.bfloat16)
            weighted_ref[t, pl.ds(s * TILE, TILE), :] = raw[0, 0, pl.ds(s * TILE, TILE), pl.ds(t * TILE, TILE)] * keep
    for s in range(RING + 1):
        ends = []
        for n in range(2):
            copies[s][n].wait()
            pack_ref[s, (4 + n) * HT : (5 + n) * HT, :] = stage[s, n, :HT, HT:]
            first = stage[s, n, :HT, :HT].astype(jnp.float32)
            second = stage[s, n, HT:, HT:].astype(jnp.float32)
            pack_ref[s, (6 + n) * HT : (7 + n) * HT, :] = jnp.where(row <= col, first, second).astype(jnp.bfloat16)
            ends.append(jnp.sum(jnp.where(row == col, second, 0.0), axis=0, keepdims=True))
        pack_ref[s, 8 * HT :, :] = jnp.where(line == 0, ends[0], ends[1]).astype(jnp.bfloat16)
    for s in range(RING + 1):
        for n in range(2, 4):
            copies[s][n].wait()


def ladder_kernel(
    pack_ref, weighted_ref, out_ref,
    slots, extra, through, factor, inputs, inner, total, give, got, pass_on, passed,
    f_send, f_recv, x_send, x_recv, r_send, r_recv, w_send, w_recv, p_send, p_recv, m_send, m_recv,
):
    i = lax.axis_index("orow")
    j = lax.axis_index("ocol")
    half = j // RING
    me = j - half * RING
    y, core = me // 2, me % 2
    fi, fj = flip(i), flip(j)
    same = i // RING == half
    diag = i == j
    lower = jnp.logical_and(same, gives(i, j))
    upper = jnp.logical_and(same, gives(j, i))
    not_lower = jnp.logical_not(lower)
    not_upper = jnp.logical_not(upper)
    swapped = jnp.logical_or(upper, diag)
    dflag = jnp.where(diag, 1, 0)
    w_dev = (jnp.where(swapped, fj, j), jnp.where(swapped, fi, i))
    p_swap = jnp.logical_or(lower, diag)
    p_dev = (jnp.where(p_swap, fj, j), jnp.where(p_swap, fi, i))
    m_dev = (fi, fj)
    t_dev = (j, i)

    def peer(k):
        step = k // 2
        dy = step + step // 2 - 2 * (step // 3)
        return ((y + dy) % 4) * 2 + (core + k) % 2

    entry = (i // 2) % 4
    ahead = entry % 2 == 0
    place = (y - entry + 4) % 4
    detours = jnp.logical_or(place == 0, place == jnp.where(ahead, 1, 3))
    relays = jnp.logical_not(detours)
    via = (y + jnp.where(jnp.logical_xor(place == 0, ahead), 1, 3)) % 4
    origin = (y + jnp.where(jnp.logical_xor(place == 2, ahead), 1, 3)) % 4

    barrier = pltpu.get_barrier_semaphore()

    def greet(device):
        pl.semaphore_signal(barrier, inc=1, device_id=device, device_id_type=MESH)

    for k in range(1, RING):
        greet((i, half * RING + peer(k)))
    greet(w_dev)

    @pl.when(jnp.logical_or(upper, lower))
    def _():
        greet(p_dev)

    @pl.when(lower)
    def _():
        greet(m_dev)

    pl.semaphore_wait(barrier, RING + jnp.where(diag, 0, jnp.where(same, 1, 0)) + jnp.where(lower, 1, 0))

    def remote(src, dst, send, recv, device):
        return pltpu.make_async_remote_copy(
            src_ref=src, dst_ref=dst, send_sem=send, recv_sem=recv, device_id=device, device_id_type=MESH
        )

    def w_copy(h):
        return remote(weighted_ref.at[h], inputs.at[1, h], w_send.at[1, h], w_recv.at[1, h], w_dev)

    def w_more(h):
        return remote(weighted_ref.at[h], inputs.at[0, h], w_send.at[0, h], w_recv.at[0, h], m_dev)

    def w_own(h):
        return pltpu.make_async_copy(weighted_ref.at[h], inputs.at[0, h], w_recv.at[0, h])

    lead = leads(i, j)
    w_first = jnp.logical_or(upper, jnp.logical_and(lead, jnp.logical_not(same)))
    w_held = jnp.logical_not(w_first)

    @pl.when(w_first)
    def _():
        for h in range(2):
            w_copy(h).start()

    for h in range(2):

        @pl.when(lower)
        def _():
            w_more(h).start()

        @pl.when(not_lower)
        def _():
            w_own(h).start()

    def leading(k):
        return leads(i, half * RING + peer(k))

    def f_copy(k):
        to = peer(k)
        return remote(pack_ref.at[to], slots.at[me], f_send.at[k], f_recv.at[me], (i, half * RING + to))

    def detour(n):
        to = peer(RING - 2 + n)
        return remote(
            pack_ref.at[to], through.at[n], f_send.at[RING - 2 + n], r_recv.at[n], (i, half * RING + via * 2 + core)
        )

    def forward(n):
        at = origin * 2 + core
        to = half * RING + (origin + 2) % 4 * 2 + (core + n) % 2
        return remote(through.at[n], slots.at[at], r_send.at[n], f_recv.at[at], (i, to))

    f_own = pltpu.make_async_copy(pack_ref.at[me], slots.at[me], f_send.at[0])
    f_own.start()
    x_copy = remote(pack_ref.at[RING], extra.at[me], x_send.at[0], x_recv.at[me], (i, i))
    x_own = pltpu.make_async_copy(pack_ref.at[RING], extra.at[me], x_send.at[1])
    def send_factors(first):
        for n in range(2):

            @pl.when(jnp.logical_and(detours, leading(RING - 2 + n) == first))
            def _():
                detour(n).start()

        for k in range(1, RING):

            @pl.when(jnp.logical_and(leading(k) == first, relays if k >= RING - 2 else True))
            def _():
                f_copy(k).start()

    send_factors(True)
    send_factors(False)

    @pl.when(jnp.logical_and(same, jnp.logical_not(diag)))
    def _():
        x_copy.start()

    @pl.when(diag)
    def _():
        x_own.start()

    total[...] = jnp.zeros_like(total)

    @pl.when(w_held)
    def _():
        for k in range(1, RING):

            @pl.when(leading(k))
            def _():
                f_copy(k).wait_send()

        for h in range(2):
            w_copy(h).start()

    @pl.when(not_lower)
    def _():
        for h in range(2):
            w_own(h).wait()

    f_own.wait()

    @pl.when(diag)
    def _():
        x_own.wait()

    row, col = corner()

    def build(source, slot, which):
        for n in range(2):
            at = n * TILE
            side = source[slot, 4 * HT + n * HT : 5 * HT + n * HT, :]
            mixed = source[slot, 6 * HT + n * HT : 7 * HT + n * HT, :].astype(jnp.float32)
            turned = mixed.T
            ends = source[slot, 8 * HT :, :].astype(jnp.float32)[n : n + 1, :]
            factor[which, at : at + HT, at : at + HT] = jnp.where(row <= col, mixed, turned).astype(jnp.bfloat16)
            factor[which, at : at + HT, at + HT : at + TILE] = side
            factor[which, at + HT : at + TILE, at : at + HT] = side.T
            factor[which, at + HT : at + TILE, at + HT : at + TILE] = jnp.where(
                row > col, mixed, jnp.where(row == col, ends, turned)
            ).astype(jnp.bfloat16)
            block = source[slot, n * TILE : n * TILE + TILE, :]
            factor[which, :TILE, TILE + n * HT : TILE + n * HT + HT] = block
            factor[which, TILE + n * HT : TILE + n * HT + HT, :TILE] = block.T

    def add(side, which):
        for h in range(2):
            inner[:, h * TILE : h * TILE + TILE] = jnp.dot(
                factor[which], inputs[side, h], preferred_element_type=jnp.float32
            ).astype(jnp.bfloat16)
        for c in range(2):
            cols = pl.ds(c * TILE, TILE)
            total[side, :, cols] += jnp.dot(
                inner[...], factor[which, :, cols], preferred_element_type=jnp.float32
            )

    def again(n, carry):
        add(1, n + RING * dflag)
        return carry

    def step(k, carry):
        slot = peer(k)

        @pl.when(k == LATE)
        def _():
            for h in range(2):
                w_copy(h).wait_recv()
            lax.fori_loop(0, LATE, again, 0)

        @pl.when(jnp.logical_and(lower, k == SOON))
        def _():
            for h in range(2):
                w_more(h).wait_recv()
            for n in range(SOON):
                add(0, n)

        for n in range(2):
            first = leads(i, half * RING + (origin + 2) % 4 * 2 + (core + n) % 2)

            @pl.when(jnp.logical_and(relays, k == jnp.where(first, 1, REST)))
            def _():
                detour(n).wait_recv()
                forward(n).start()

        @pl.when(k > 0)
        def _():
            remote(pack_ref.at[slot], slots.at[slot], f_send.at[slot], f_recv.at[slot], w_dev).wait_recv()

        build(slots, slot, k)

        @pl.when(diag)
        def _():
            @pl.when(k > 0)
            def _():
                remote(pack_ref.at[RING], extra.at[slot], x_send.at[0], x_recv.at[slot], w_dev).wait_recv()

            build(extra, slot, k + RING)

        @pl.when(jnp.logical_or(not_lower, k >= SOON))
        def _():
            add(0, k)

        lax.fori_loop(k, jnp.where(k < LATE, k, k + 1), again, 0)
        return carry

    lax.fori_loop(0, RING, step, 0)

    def p_copy(r):
        return remote(give.at[r], got.at[r], p_send.at[r], p_recv.at[r], p_dev)

    def m_copy(r):
        return remote(pass_on.at[r], passed.at[r], m_send.at[r], m_recv.at[r], t_dev)

    @pl.when(not_upper)
    def _():
        for r in range(CHUNKS):
            rows = pl.ds(r * ROWS, ROWS)
            ours = (total[1, rows, :] + total[dflag, :, rows].T).astype(jnp.bfloat16)
            for n in range(2):
                give[2 * r + n] = ours[n * PART : (n + 1) * PART]
                p_copy(2 * r + n).start()

    @pl.when(not_lower)
    def _():
        for r in range(CHUNKS):
            rows = pl.ds(r * ROWS, ROWS)
            out_ref[rows, :] = total[0, rows, :] + total[1 - dflag, :, rows].T
        for r in range(SENDS):
            rows = pl.ds(r * PART, PART)
            p_copy(r).wait_recv()
            ours = out_ref[rows, :] + got[r].astype(jnp.float32)
            out_ref[rows, :] = ours

            @pl.when(upper)
            def _():
                pass_on[r] = ours.astype(jnp.bfloat16)
                m_copy(r).start()

    @pl.when(lower)
    def _():
        for r in range(CHUNKS):
            for n in range(2):
                m_copy(2 * r + n).wait_recv()
            both = jnp.concatenate([passed[2 * r], passed[2 * r + 1]], axis=0)
            out_ref[:, pl.ds(r * ROWS, ROWS)] = both.astype(jnp.float32).T

    for h in range(2):
        w_copy(h).wait_send()
    for k in range(1, RING):

        @pl.when(jnp.logical_not(jnp.logical_and(w_held, leading(k))))
        def _():
            f_copy(k).wait_send()

    @pl.when(relays)
    def _():
        for n in range(2):
            forward(n).wait_send()

    @pl.when(not_upper)
    def _():
        for r in range(SENDS):
            p_copy(r).wait_send()

    @pl.when(upper)
    def _():
        for r in range(SENDS):
            m_copy(r).wait_send()

    @pl.when(jnp.logical_and(same, jnp.logical_not(diag)))
    def _():
        x_copy.wait_send()

    @pl.when(lower)
    def _():
        for h in range(2):
            w_more(h).wait_send()


def shards(amplitudes, tile_mask, domain_tiles, cholesky):
    vmem = pl.BlockSpec(memory_space=pltpu.VMEM)
    smem = pl.BlockSpec(memory_space=pltpu.SMEM)
    hbm = pl.BlockSpec(memory_space=pl.ANY)
    dma = pltpu.SemaphoreType.DMA
    half = jnp.bfloat16
    pack, weighted = pl.pallas_call(
        prep_kernel,
        out_shape=(
            pltpu.VMEM((RING + 1, PACK, HT), half),
            pltpu.VMEM((2, DV, TILE), half),
        ),
        in_specs=[smem, smem, hbm, hbm],
        out_specs=(vmem, vmem),
        scratch_shapes=[
            pltpu.VMEM((RING + 1, 2, TILE, TILE), half),
            pltpu.VMEM((1, 1, DV, DV), half),
            dma((RING + 1, 4)),
            dma,
        ],
        compiler_params=pltpu.CompilerParams(vmem_limit_bytes=56 << 20),
        name="prep",
    )(domain_tiles.transpose(0, 2, 1), tile_mask, amplitudes, cholesky)
    ladder = pl.pallas_call(
        ladder_kernel,
        out_shape=jax.ShapeDtypeStruct((DV, DV), jnp.float32),
        in_specs=[vmem, vmem],
        out_specs=vmem,
        scratch_shapes=[
            pltpu.VMEM((RING, PACK, HT), half),
            pltpu.VMEM((RING, PACK, HT), half),
            pltpu.VMEM((2, PACK, HT), half),
            pltpu.VMEM((2 * RING, DV, DV), half),
            pltpu.VMEM((2, 2, DV, TILE), half),
            pltpu.VMEM((DV, DV), half),
            pltpu.VMEM((2, DV, DV), jnp.float32),
            pltpu.VMEM((SENDS, PART, DV), half),
            pltpu.VMEM((SENDS, PART, DV), half),
            pltpu.VMEM((SENDS, PART, DV), half),
            pltpu.VMEM((SENDS, PART, DV), half),
            dma((RING,)), dma((RING,)), dma((2,)), dma((RING,)), dma((2,)), dma((2,)), dma((2, 2)), dma((2, 2)),
            dma((SENDS,)), dma((SENDS,)), dma((SENDS,)), dma((SENDS,)),
        ],
        compiler_params=pltpu.CompilerParams(
            collective_id=0, has_side_effects=True, vmem_limit_bytes=36 << 20
        ),
        name="ladder",
    )(pack, weighted)
    return ladder.reshape(1, 1, DV, DV)


def solution(mesh):
    return jax.shard_map(
        shards,
        mesh=mesh,
        in_specs=(
            P("orow", "ocol", None, None),
            P("orow", "ocol", None, None),
            P(),
            P("ocol", None, None),
        ),
        out_specs=P("orow", "ocol", None, None),
        check_vma=False,
    )
```

```python
import jax
import jax.numpy as jnp
from jax import lax
from jax.experimental import pallas as pl
from jax.experimental.pallas import tpu as pltpu
from jax.sharding import PartitionSpec as P

TILE = 256
HT = 128
DV = 512
NO = 16
RING = 8
CHUNKS = 4
SENDS = 8
REST = 5
SOON = 4
LATE = 5
ROWS = DV // CHUNKS
PART = DV // SENDS
PACK = 8 * HT + 16
MESH = pl.DeviceIdType.MESH


def flip(index):
    return index + RING - 2 * RING * (index // RING)


def gives(i, j):
    even = (i // 4 + j // 4 + i + j) % 2 == 0
    return jnp.logical_or(jnp.logical_and(i > j, jnp.logical_not(even)), jnp.logical_and(i < j, even))


def leads(i, j):
    near = i // RING == j // RING
    return jnp.logical_or(
        jnp.logical_and(near, gives(i, j)), jnp.logical_and(jnp.logical_not(near), (i + j) % 2 == 0)
    )


def corner(shape=(HT, HT)):
    return lax.broadcasted_iota(jnp.int32, shape, 0), lax.broadcasted_iota(jnp.int32, shape, 1)


def prep_kernel(tiles_ref, mask_ref, amp_ref, chol_ref, pack_ref, weighted_ref, stage, raw, sems, raw_sem):
    i = lax.axis_index("orow")
    half = lax.axis_index("ocol") // RING
    raw_copy = pltpu.make_async_copy(amp_ref, raw, raw_sem)
    copies = []
    for s in range(RING + 1):
        if s < RING:
            j = half * RING + s
            other = jnp.logical_and(i // RING == half, gives(i, j))
            a = jnp.where(other, flip(i), i)
            b = jnp.where(other, flip(j), j)
        else:
            a = b = flip(i)
        t0 = tiles_ref[a, 0, b] * TILE
        t1 = tiles_ref[a, 1, b] * TILE

        def pick(row, col, width, dst, sem):
            copy = pltpu.make_async_copy(
                chol_ref.at[0, pl.ds(pl.multiple_of(row, TILE), TILE), pl.ds(pl.multiple_of(col, HT), width)], dst, sem
            )
            copy.start()
            return copy

        mine = [pick(t, t, TILE, stage.at[s, n], sems.at[s, n]) for n, t in enumerate((t0, t1))]
        for n in range(2):
            mine.append(pick(t0, t1 + n * HT, HT, pack_ref.at[s, pl.ds(n * TILE, TILE)], sems.at[s, 2 + n]))
        copies.append(mine)
        if s == 0:
            raw_copy.start()
    row, col = corner()
    line = lax.broadcasted_iota(jnp.int32, (16, HT), 0)
    raw_copy.wait()
    for s in range(2):
        for t in range(2):
            keep = mask_ref[0, 0, s, t].astype(jnp.float32).astype(jnp.bfloat16)
            weighted_ref[t, pl.ds(s * TILE, TILE), :] = raw[0, 0, pl.ds(s * TILE, TILE), pl.ds(t * TILE, TILE)] * keep
    for s in range(RING + 1):
        ends = []
        for n in range(2):
            copies[s][n].wait()
            pack_ref[s, (4 + n) * HT : (5 + n) * HT, :] = stage[s, n, :HT, HT:]
            first = stage[s, n, :HT, :HT].astype(jnp.float32)
            second = stage[s, n, HT:, HT:].astype(jnp.float32)
            pack_ref[s, (6 + n) * HT : (7 + n) * HT, :] = jnp.where(row <= col, first, second).astype(jnp.bfloat16)
            ends.append(jnp.sum(jnp.where(row == col, second, 0.0), axis=0, keepdims=True))
        pack_ref[s, 8 * HT :, :] = jnp.where(line == 0, ends[0], ends[1]).astype(jnp.bfloat16)
    for s in range(RING + 1):
        for n in range(2, 4):
            copies[s][n].wait()


def ladder_kernel(
    pack_ref, weighted_ref, out_ref,
    slots, extra, through, factor, inputs, inner, total, give, got, pass_on, passed,
    f_send, f_recv, x_send, x_recv, r_send, r_recv, w_send, w_recv, p_send, p_recv, m_send, m_recv,
):
    i = lax.axis_index("orow")
    j = lax.axis_index("ocol")
    half = j // RING
    me = j - half * RING
    y, core = me // 2, me % 2
    fi, fj = flip(i), flip(j)
    same = i // RING == half
    diag = i == j
    lower = jnp.logical_and(same, gives(i, j))
    upper = jnp.logical_and(same, gives(j, i))
    not_lower = jnp.logical_not(lower)
    not_upper = jnp.logical_not(upper)
    swapped = jnp.logical_or(upper, diag)
    dflag = jnp.where(diag, 1, 0)
    w_dev = (jnp.where(swapped, fj, j), jnp.where(swapped, fi, i))
    p_swap = jnp.logical_or(lower, diag)
    p_dev = (jnp.where(p_swap, fj, j), jnp.where(p_swap, fi, i))
    m_dev = (fi, fj)
    t_dev = (j, i)

    def peer(k):
        step = k // 2
        dy = step + step // 2 - 2 * (step // 3)
        return ((y + dy) % 4) * 2 + (core + k) % 2

    entry = (i // 2) % 4
    ahead = entry % 2 == 0
    place = (y - entry + 4) % 4
    detours = jnp.logical_or(place == 0, place == jnp.where(ahead, 1, 3))
    relays = jnp.logical_not(detours)
    via = (y + jnp.where(jnp.logical_xor(place == 0, ahead), 1, 3)) % 4
    origin = (y + jnp.where(jnp.logical_xor(place == 2, ahead), 1, 3)) % 4

    barrier = pltpu.get_barrier_semaphore()

    def greet(device):
        pl.semaphore_signal(barrier, inc=1, device_id=device, device_id_type=MESH)

    for k in range(1, RING):
        greet((i, half * RING + peer(k)))
    greet(w_dev)

    @pl.when(jnp.logical_or(upper, lower))
    def _():
        greet(p_dev)

    @pl.when(lower)
    def _():
        greet(m_dev)

    pl.semaphore_wait(barrier, RING + jnp.where(diag, 0, jnp.where(same, 1, 0)) + jnp.where(lower, 1, 0))

    def remote(src, dst, send, recv, device):
        return pltpu.make_async_remote_copy(
            src_ref=src, dst_ref=dst, send_sem=send, recv_sem=recv, device_id=device, device_id_type=MESH
        )

    def w_copy(h):
        return remote(weighted_ref.at[h], inputs.at[1, h], w_send.at[1, h], w_recv.at[1, h], w_dev)

    def w_more(h):
        return remote(weighted_ref.at[h], inputs.at[0, h], w_send.at[0, h], w_recv.at[0, h], m_dev)

    def w_own(h):
        return pltpu.make_async_copy(weighted_ref.at[h], inputs.at[0, h], w_recv.at[0, h])

    lead = leads(i, j)
    w_first = jnp.logical_or(upper, jnp.logical_and(lead, jnp.logical_not(same)))
    w_held = jnp.logical_not(w_first)

    @pl.when(w_first)
    def _():
        for h in range(2):
            w_copy(h).start()

    for h in range(2):

        @pl.when(lower)
        def _():
            w_more(h).start()

        @pl.when(not_lower)
        def _():
            w_own(h).start()

    def leading(k):
        return leads(i, half * RING + peer(k))

    def f_copy(k):
        to = peer(k)
        return remote(pack_ref.at[to], slots.at[me], f_send.at[k], f_recv.at[me], (i, half * RING + to))

    def detour(n):
        to = peer(RING - 2 + n)
        return remote(
            pack_ref.at[to], through.at[n], f_send.at[RING - 2 + n], r_recv.at[n], (i, half * RING + via * 2 + core)
        )

    def forward(n):
        at = origin * 2 + core
        to = half * RING + (origin + 2) % 4 * 2 + (core + n) % 2
        return remote(through.at[n], slots.at[at], r_send.at[n], f_recv.at[at], (i, to))

    f_own = pltpu.make_async_copy(pack_ref.at[me], slots.at[me], f_send.at[0])
    f_own.start()
    x_copy = remote(pack_ref.at[RING], extra.at[me], x_send.at[0], x_recv.at[me], (i, i))
    x_own = pltpu.make_async_copy(pack_ref.at[RING], extra.at[me], x_send.at[1])
    def send_factors(first):
        for n in range(2):

            @pl.when(jnp.logical_and(detours, leading(RING - 2 + n) == first))
            def _():
                detour(n).start()

        for k in range(1, RING):

            @pl.when(jnp.logical_and(leading(k) == first, relays if k >= RING - 2 else True))
            def _():
                f_copy(k).start()

    send_factors(True)
    send_factors(False)

    @pl.when(jnp.logical_and(same, jnp.logical_not(diag)))
    def _():
        x_copy.start()

    @pl.when(diag)
    def _():
        x_own.start()

    total[...] = jnp.zeros_like(total)

    @pl.when(w_held)
    def _():
        for k in range(1, RING):

            @pl.when(leading(k))
            def _():
                f_copy(k).wait_send()

        for h in range(2):
            w_copy(h).start()

    @pl.when(not_lower)
    def _():
        for h in range(2):
            w_own(h).wait()

    f_own.wait()

    @pl.when(diag)
    def _():
        x_own.wait()

    row, col = corner()

    def build(source, slot, which):
        for n in range(2):
            at = n * TILE
            side = source[slot, 4 * HT + n * HT : 5 * HT + n * HT, :]
            mixed = source[slot, 6 * HT + n * HT : 7 * HT + n * HT, :].astype(jnp.float32)
            turned = mixed.T
            ends = source[slot, 8 * HT :, :].astype(jnp.float32)[n : n + 1, :]
            factor[which, at : at + HT, at : at + HT] = jnp.where(row <= col, mixed, turned).astype(jnp.bfloat16)
            factor[which, at : at + HT, at + HT : at + TILE] = side
            factor[which, at + HT : at + TILE, at : at + HT] = side.T
            factor[which, at + HT : at + TILE, at + HT : at + TILE] = jnp.where(
                row > col, mixed, jnp.where(row == col, ends, turned)
            ).astype(jnp.bfloat16)
            block = source[slot, n * TILE : n * TILE + TILE, :]
            factor[which, :TILE, TILE + n * HT : TILE + n * HT + HT] = block
            factor[which, TILE + n * HT : TILE + n * HT + HT, :TILE] = block.T

    def add(side, which):
        for h in range(2):
            inner[:, h * TILE : h * TILE + TILE] = jnp.dot(
                factor[which], inputs[side, h], preferred_element_type=jnp.float32
            ).astype(jnp.bfloat16)
        for c in range(2):
            cols = pl.ds(c * TILE, TILE)
            total[side, :, cols] += jnp.dot(
                inner[...], factor[which, :, cols], preferred_element_type=jnp.float32
            )

    def again(n, carry):
        add(1, n + RING * dflag)
        return carry

    def step(k, carry):
        slot = peer(k)

        @pl.when(k == LATE)
        def _():
            for h in range(2):
                w_copy(h).wait_recv()
            lax.fori_loop(0, LATE, again, 0)

        @pl.when(jnp.logical_and(lower, k == SOON))
        def _():
            for h in range(2):
                w_more(h).wait_recv()
            for n in range(SOON):
                add(0, n)

        for n in range(2):
            first = leads(i, half * RING + (origin + 2) % 4 * 2 + (core + n) % 2)

            @pl.when(jnp.logical_and(relays, k == jnp.where(first, 1, REST)))
            def _():
                detour(n).wait_recv()
                forward(n).start()

        @pl.when(k > 0)
        def _():
            remote(pack_ref.at[slot], slots.at[slot], f_send.at[slot], f_recv.at[slot], w_dev).wait_recv()

        build(slots, slot, k)

        @pl.when(diag)
        def _():
            @pl.when(k > 0)
            def _():
                remote(pack_ref.at[RING], extra.at[slot], x_send.at[0], x_recv.at[slot], w_dev).wait_recv()

            build(extra, slot, k + RING)

        @pl.when(jnp.logical_or(not_lower, k >= SOON))
        def _():
            add(0, k)

        lax.fori_loop(k, jnp.where(k < LATE, k, k + 1), again, 0)
        return carry

    lax.fori_loop(0, RING, step, 0)

    def p_copy(r):
        return remote(give.at[r], got.at[r], p_send.at[r], p_recv.at[r], p_dev)

    def m_copy(r):
        return remote(pass_on.at[r], passed.at[r], m_send.at[r], m_recv.at[r], t_dev)

    @pl.when(not_upper)
    def _():
        for r in range(CHUNKS):
            rows = pl.ds(r * ROWS, ROWS)
            ours = (total[1, rows, :] + total[dflag, :, rows].T).astype(jnp.bfloat16)
            for n in range(2):
                give[2 * r + n] = ours[n * PART : (n + 1) * PART]
                p_copy(2 * r + n).start()

    @pl.when(not_lower)
    def _():
        for r in range(CHUNKS):
            rows = pl.ds(r * ROWS, ROWS)
            out_ref[rows, :] = total[0, rows, :] + total[1 - dflag, :, rows].T
        for r in range(SENDS):
            rows = pl.ds(r * PART, PART)
            p_copy(r).wait_recv()
            ours = out_ref[rows, :] + got[r].astype(jnp.float32)
            out_ref[rows, :] = ours

            @pl.when(upper)
            def _():
                pass_on[r] = ours.astype(jnp.bfloat16)
                m_copy(r).start()

    @pl.when(lower)
    def _():
        for r in range(CHUNKS):
            for n in range(2):
                m_copy(2 * r + n).wait_recv()
            both = jnp.concatenate([passed[2 * r], passed[2 * r + 1]], axis=0)
            out_ref[:, pl.ds(r * ROWS, ROWS)] = both.astype(jnp.float32).T

    for h in range(2):
        w_copy(h).wait_send()
    for k in range(1, RING):

        @pl.when(jnp.logical_not(jnp.logical_and(w_held, leading(k))))
        def _():
            f_copy(k).wait_send()

    @pl.when(relays)
    def _():
        for n in range(2):
            forward(n).wait_send()

    @pl.when(not_upper)
    def _():
        for r in range(SENDS):
            p_copy(r).wait_send()

    @pl.when(upper)
    def _():
        for r in range(SENDS):
            m_copy(r).wait_send()

    @pl.when(jnp.logical_and(same, jnp.logical_not(diag)))
    def _():
        x_copy.wait_send()

    @pl.when(lower)
    def _():
        for h in range(2):
            w_more(h).wait_send()


def shards(amplitudes, tile_mask, domain_tiles, cholesky):
    vmem = pl.BlockSpec(memory_space=pltpu.VMEM)
    smem = pl.BlockSpec(memory_space=pltpu.SMEM)
    hbm = pl.BlockSpec(memory_space=pl.ANY)
    dma = pltpu.SemaphoreType.DMA
    half = jnp.bfloat16
    pack, weighted = pl.pallas_call(
        prep_kernel,
        out_shape=(
            pltpu.VMEM((RING + 1, PACK, HT), half),
            pltpu.VMEM((2, DV, TILE), half),
        ),
        in_specs=[smem, smem, hbm, hbm],
        out_specs=(vmem, vmem),
        scratch_shapes=[
            pltpu.VMEM((RING + 1, 2, TILE, TILE), half),
            pltpu.VMEM((1, 1, DV, DV), half),
            dma((RING + 1, 4)),
            dma,
        ],
        compiler_params=pltpu.CompilerParams(vmem_limit_bytes=56 << 20),
        name="prep",
    )(domain_tiles.transpose(0, 2, 1), tile_mask, amplitudes, cholesky)
    ladder = pl.pallas_call(
        ladder_kernel,
        out_shape=jax.ShapeDtypeStruct((DV, DV), jnp.float32),
        in_specs=[vmem, vmem],
        out_specs=vmem,
        scratch_shapes=[
            pltpu.VMEM((RING, PACK, HT), half),
            pltpu.VMEM((RING, PACK, HT), half),
            pltpu.VMEM((2, PACK, HT), half),
            pltpu.VMEM((2 * RING, DV, DV), half),
            pltpu.VMEM((2, 2, DV, TILE), half),
            pltpu.VMEM((DV, DV), half),
            pltpu.VMEM((2, DV, DV), jnp.float32),
            pltpu.VMEM((SENDS, PART, DV), half),
            pltpu.VMEM((SENDS, PART, DV), half),
            pltpu.VMEM((SENDS, PART, DV), half),
            pltpu.VMEM((SENDS, PART, DV), half),
            dma((RING,)), dma((RING,)), dma((2,)), dma((RING,)), dma((2,)), dma((2,)), dma((2, 2)), dma((2, 2)),
            dma((SENDS,)), dma((SENDS,)), dma((SENDS,)), dma((SENDS,)),
        ],
        compiler_params=pltpu.CompilerParams(
            collective_id=0, has_side_effects=True, vmem_limit_bytes=36 << 20
        ),
        name="ladder",
    )(pack, weighted)
    return ladder.reshape(1, 1, DV, DV)


def solution(mesh):
    return jax.shard_map(
        shards,
        mesh=mesh,
        in_specs=(
            P("orow", "ocol", None, None),
            P("orow", "ocol", None, None),
            P(),
            P("ocol", None, None),
        ),
        out_specs=P("orow", "ocol", None, None),
        check_vma=False,
    )
```

```python
import jax
import jax.numpy as jnp
from jax import lax
from jax.experimental import pallas as pl
from jax.experimental.pallas import tpu as pltpu
from jax.sharding import PartitionSpec as P

TILE = 256
HT = 128
DV = 512
NO = 16
RING = 8
CHUNKS = 4
SENDS = 8
REST = 5
SOON = 4
LATE = 5
ROWS = DV // CHUNKS
PART = DV // SENDS
PACK = 8 * HT + 16
MESH = pl.DeviceIdType.MESH


def flip(index):
    return index + RING - 2 * RING * (index // RING)


def gives(i, j):
    even = (i // 4 + j // 4 + i + j) % 2 == 0
    return jnp.logical_or(jnp.logical_and(i > j, jnp.logical_not(even)), jnp.logical_and(i < j, even))


def leads(i, j):
    near = i // RING == j // RING
    return jnp.logical_or(
        jnp.logical_and(near, gives(i, j)), jnp.logical_and(jnp.logical_not(near), (i + j) % 2 == 0)
    )


def corner(shape=(HT, HT)):
    return lax.broadcasted_iota(jnp.int32, shape, 0), lax.broadcasted_iota(jnp.int32, shape, 1)


def prep_kernel(tiles_ref, mask_ref, amp_ref, chol_ref, pack_ref, weighted_ref, stage, raw, sems, raw_sem):
    i = lax.axis_index("orow")
    half = lax.axis_index("ocol") // RING
    raw_copy = pltpu.make_async_copy(amp_ref, raw, raw_sem)
    def pick(row, col, width, dst, sem):
        copy = pltpu.make_async_copy(
            chol_ref.at[0, pl.ds(pl.multiple_of(row, TILE), TILE), pl.ds(pl.multiple_of(col, HT), width)], dst, sem
        )
        copy.start()
        return copy

    copies, corners = [], []
    for s in range(RING + 1):
        if s < RING:
            j = half * RING + s
            other = jnp.logical_and(i // RING == half, gives(i, j))
            a = jnp.where(other, flip(i), i)
            b = jnp.where(other, flip(j), j)
        else:
            a = b = flip(i)
        t0 = tiles_ref[a, 0, b] * TILE
        t1 = tiles_ref[a, 1, b] * TILE

        mine = [pick(t, t, TILE, stage.at[s, n], sems.at[s, n]) for n, t in enumerate((t0, t1))]
        copies.append(mine)
        corners.append((t0, t1))
    raw_copy.start()
    for s, (t0, t1) in enumerate(corners):
        for n in range(2):
            copies[s].append(pick(t0, t1 + n * HT, HT, pack_ref.at[s, pl.ds(n * TILE, TILE)], sems.at[s, 2 + n]))
    row, col = corner()
    line = lax.broadcasted_iota(jnp.int32, (16, HT), 0)
    for s in range(RING + 1):
        ends = []
        for n in range(2):
            copies[s][n].wait()
            pack_ref[s, (4 + n) * HT : (5 + n) * HT, :] = stage[s, n, :HT, HT:]
            first = stage[s, n, :HT, :HT].astype(jnp.float32)
            second = stage[s, n, HT:, HT:].astype(jnp.float32)
            pack_ref[s, (6 + n) * HT : (7 + n) * HT, :] = jnp.where(row <= col, first, second).astype(jnp.bfloat16)
            ends.append(jnp.sum(jnp.where(row == col, second, 0.0), axis=0, keepdims=True))
        pack_ref[s, 8 * HT :, :] = jnp.where(line == 0, ends[0], ends[1]).astype(jnp.bfloat16)
    raw_copy.wait()
    for s in range(2):
        for t in range(2):
            keep = mask_ref[0, 0, s, t].astype(jnp.float32).astype(jnp.bfloat16)
            weighted_ref[t, pl.ds(s * TILE, TILE), :] = raw[0, 0, pl.ds(s * TILE, TILE), pl.ds(t * TILE, TILE)] * keep
    for s in range(RING + 1):
        for n in range(2, 4):
            copies[s][n].wait()


def ladder_kernel(
    pack_ref, weighted_ref, out_ref,
    slots, extra, through, factor, inputs, inner, total, give, got, pass_on, passed,
    f_send, f_recv, x_send, x_recv, r_send, r_recv, w_send, w_recv, p_send, p_recv, m_send, m_recv,
):
    i = lax.axis_index("orow")
    j = lax.axis_index("ocol")
    half = j // RING
    me = j - half * RING
    y, core = me // 2, me % 2
    fi, fj = flip(i), flip(j)
    same = i // RING == half
    diag = i == j
    lower = jnp.logical_and(same, gives(i, j))
    upper = jnp.logical_and(same, gives(j, i))
    not_lower = jnp.logical_not(lower)
    not_upper = jnp.logical_not(upper)
    swapped = jnp.logical_or(upper, diag)
    dflag = jnp.where(diag, 1, 0)
    w_dev = (jnp.where(swapped, fj, j), jnp.where(swapped, fi, i))
    p_swap = jnp.logical_or(lower, diag)
    p_dev = (jnp.where(p_swap, fj, j), jnp.where(p_swap, fi, i))
    m_dev = (fi, fj)
    t_dev = (j, i)

    def peer(k):
        step = k // 2
        dy = step + step // 2 - 2 * (step // 3)
        return ((y + dy) % 4) * 2 + (core + k) % 2

    entry = (i // 2) % 4
    ahead = entry % 2 == 0
    place = (y - entry + 4) % 4
    detours = jnp.logical_or(place == 0, place == jnp.where(ahead, 1, 3))
    relays = jnp.logical_not(detours)
    via = (y + jnp.where(jnp.logical_xor(place == 0, ahead), 1, 3)) % 4
    origin = (y + jnp.where(jnp.logical_xor(place == 2, ahead), 1, 3)) % 4

    barrier = pltpu.get_barrier_semaphore()

    def greet(device):
        pl.semaphore_signal(barrier, inc=1, device_id=device, device_id_type=MESH)

    for k in range(1, RING):
        greet((i, half * RING + peer(k)))
    greet(w_dev)

    @pl.when(jnp.logical_or(upper, lower))
    def _():
        greet(p_dev)

    @pl.when(lower)
    def _():
        greet(m_dev)

    pl.semaphore_wait(barrier, RING + jnp.where(diag, 0, jnp.where(same, 1, 0)) + jnp.where(lower, 1, 0))

    def remote(src, dst, send, recv, device):
        return pltpu.make_async_remote_copy(
            src_ref=src, dst_ref=dst, send_sem=send, recv_sem=recv, device_id=device, device_id_type=MESH
        )

    def w_copy(h):
        return remote(weighted_ref.at[h], inputs.at[1, h], w_send.at[1, h], w_recv.at[1, h], w_dev)

    def w_more(h):
        return remote(weighted_ref.at[h], inputs.at[0, h], w_send.at[0, h], w_recv.at[0, h], m_dev)

    def w_own(h):
        return pltpu.make_async_copy(weighted_ref.at[h], inputs.at[0, h], w_recv.at[0, h])

    lead = leads(i, j)
    w_first = jnp.logical_or(upper, jnp.logical_and(lead, jnp.logical_not(same)))
    w_held = jnp.logical_not(w_first)

    @pl.when(w_first)
    def _():
        for h in range(2):
            w_copy(h).start()

    for h in range(2):

        @pl.when(lower)
        def _():
            w_more(h).start()

        @pl.when(not_lower)
        def _():
            w_own(h).start()

    def leading(k):
        return leads(i, half * RING + peer(k))

    def f_copy(k):
        to = peer(k)
        return remote(pack_ref.at[to], slots.at[me], f_send.at[k], f_recv.at[me], (i, half * RING + to))

    def detour(n):
        to = peer(RING - 2 + n)
        return remote(
            pack_ref.at[to], through.at[n], f_send.at[RING - 2 + n], r_recv.at[n], (i, half * RING + via * 2 + core)
        )

    def forward(n):
        at = origin * 2 + core
        to = half * RING + (origin + 2) % 4 * 2 + (core + n) % 2
        return remote(through.at[n], slots.at[at], r_send.at[n], f_recv.at[at], (i, to))

    f_own = pltpu.make_async_copy(pack_ref.at[me], slots.at[me], f_send.at[0])
    f_own.start()
    x_copy = remote(pack_ref.at[RING], extra.at[me], x_send.at[0], x_recv.at[me], (i, i))
    x_own = pltpu.make_async_copy(pack_ref.at[RING], extra.at[me], x_send.at[1])
    def send_factors(first):
        for n in range(2):

            @pl.when(jnp.logical_and(detours, leading(RING - 2 + n) == first))
            def _():
                detour(n).start()

        for k in range(1, RING):

            @pl.when(jnp.logical_and(leading(k) == first, relays if k >= RING - 2 else True))
            def _():
                f_copy(k).start()

    send_factors(True)
    send_factors(False)

    @pl.when(jnp.logical_and(same, jnp.logical_not(diag)))
    def _():
        x_copy.start()

    @pl.when(diag)
    def _():
        x_own.start()

    total[...] = jnp.zeros_like(total)

    @pl.when(w_held)
    def _():
        for k in range(1, RING):

            @pl.when(leading(k))
            def _():
                f_copy(k).wait_send()

        for h in range(2):
            w_copy(h).start()

    @pl.when(not_lower)
    def _():
        for h in range(2):
            w_own(h).wait()

    f_own.wait()

    @pl.when(diag)
    def _():
        x_own.wait()

    row, col = corner()

    def build(source, slot, which):
        for n in range(2):
            at = n * TILE
            side = source[slot, 4 * HT + n * HT : 5 * HT + n * HT, :]
            mixed = source[slot, 6 * HT + n * HT : 7 * HT + n * HT, :].astype(jnp.float32)
            turned = mixed.T
            ends = source[slot, 8 * HT :, :].astype(jnp.float32)[n : n + 1, :]
            factor[which, at : at + HT, at : at + HT] = jnp.where(row <= col, mixed, turned).astype(jnp.bfloat16)
            factor[which, at : at + HT, at + HT : at + TILE] = side
            factor[which, at + HT : at + TILE, at : at + HT] = side.T
            factor[which, at + HT : at + TILE, at + HT : at + TILE] = jnp.where(
                row > col, mixed, jnp.where(row == col, ends, turned)
            ).astype(jnp.bfloat16)
            block = source[slot, n * TILE : n * TILE + TILE, :]
            factor[which, :TILE, TILE + n * HT : TILE + n * HT + HT] = block
            factor[which, TILE + n * HT : TILE + n * HT + HT, :TILE] = block.T

    def add(side, which):
        for h in range(2):
            inner[:, h * TILE : h * TILE + TILE] = jnp.dot(
                factor[which], inputs[side, h], preferred_element_type=jnp.float32
            ).astype(jnp.bfloat16)
        for c in range(2):
            cols = pl.ds(c * TILE, TILE)
            total[side, :, cols] += jnp.dot(
                inner[...], factor[which, :, cols], preferred_element_type=jnp.float32
            )

    def again(n, carry):
        add(1, n + RING * dflag)
        return carry

    def step(k, carry):
        slot = peer(k)

        @pl.when(k == LATE)
        def _():
            for h in range(2):
                w_copy(h).wait_recv()
            lax.fori_loop(0, LATE, again, 0)

        @pl.when(jnp.logical_and(lower, k == SOON))
        def _():
            for h in range(2):
                w_more(h).wait_recv()
            for n in range(SOON):
                add(0, n)

        for n in range(2):
            first = leads(i, half * RING + (origin + 2) % 4 * 2 + (core + n) % 2)

            @pl.when(jnp.logical_and(relays, k == jnp.where(first, 1, REST)))
            def _():
                detour(n).wait_recv()
                forward(n).start()

        @pl.when(k > 0)
        def _():
            remote(pack_ref.at[slot], slots.at[slot], f_send.at[slot], f_recv.at[slot], w_dev).wait_recv()

        build(slots, slot, k)

        @pl.when(diag)
        def _():
            @pl.when(k > 0)
            def _():
                remote(pack_ref.at[RING], extra.at[slot], x_send.at[0], x_recv.at[slot], w_dev).wait_recv()

            build(extra, slot, k + RING)

        @pl.when(jnp.logical_or(not_lower, k >= SOON))
        def _():
            add(0, k)

        lax.fori_loop(k, jnp.where(k < LATE, k, k + 1), again, 0)
        return carry

    lax.fori_loop(0, RING, step, 0)

    def p_copy(r):
        return remote(give.at[r], got.at[r], p_send.at[r], p_recv.at[r], p_dev)

    def m_copy(r):
        return remote(pass_on.at[r], passed.at[r], m_send.at[r], m_recv.at[r], t_dev)

    @pl.when(not_upper)
    def _():
        for r in range(CHUNKS):
            rows = pl.ds(r * ROWS, ROWS)
            ours = (total[1, rows, :] + total[dflag, :, rows].T).astype(jnp.bfloat16)
            for n in range(2):
                give[2 * r + n] = ours[n * PART : (n + 1) * PART]
                p_copy(2 * r + n).start()

    @pl.when(not_lower)
    def _():
        for r in range(CHUNKS):
            rows = pl.ds(r * ROWS, ROWS)
            out_ref[rows, :] = total[0, rows, :] + total[1 - dflag, :, rows].T
        for r in range(SENDS):
            rows = pl.ds(r * PART, PART)
            p_copy(r).wait_recv()
            ours = out_ref[rows, :] + got[r].astype(jnp.float32)
            out_ref[rows, :] = ours

            @pl.when(upper)
            def _():
                pass_on[r] = ours.astype(jnp.bfloat16)
                m_copy(r).start()

    @pl.when(lower)
    def _():
        for r in range(CHUNKS):
            for n in range(2):
                m_copy(2 * r + n).wait_recv()
            both = jnp.concatenate([passed[2 * r], passed[2 * r + 1]], axis=0)
            out_ref[:, pl.ds(r * ROWS, ROWS)] = both.astype(jnp.float32).T

    for h in range(2):
        w_copy(h).wait_send()
    for k in range(1, RING):

        @pl.when(jnp.logical_not(jnp.logical_and(w_held, leading(k))))
        def _():
            f_copy(k).wait_send()

    @pl.when(relays)
    def _():
        for n in range(2):
            forward(n).wait_send()

    @pl.when(not_upper)
    def _():
        for r in range(SENDS):
            p_copy(r).wait_send()

    @pl.when(upper)
    def _():
        for r in range(SENDS):
            m_copy(r).wait_send()

    @pl.when(jnp.logical_and(same, jnp.logical_not(diag)))
    def _():
        x_copy.wait_send()

    @pl.when(lower)
    def _():
        for h in range(2):
            w_more(h).wait_send()


def shards(amplitudes, tile_mask, domain_tiles, cholesky):
    vmem = pl.BlockSpec(memory_space=pltpu.VMEM)
    smem = pl.BlockSpec(memory_space=pltpu.SMEM)
    hbm = pl.BlockSpec(memory_space=pl.ANY)
    dma = pltpu.SemaphoreType.DMA
    half = jnp.bfloat16
    pack, weighted = pl.pallas_call(
        prep_kernel,
        out_shape=(
            pltpu.VMEM((RING + 1, PACK, HT), half),
            pltpu.VMEM((2, DV, TILE), half),
        ),
        in_specs=[smem, smem, hbm, hbm],
        out_specs=(vmem, vmem),
        scratch_shapes=[
            pltpu.VMEM((RING + 1, 2, TILE, TILE), half),
            pltpu.VMEM((1, 1, DV, DV), half),
            dma((RING + 1, 4)),
            dma,
        ],
        compiler_params=pltpu.CompilerParams(vmem_limit_bytes=56 << 20),
        name="prep",
    )(domain_tiles.transpose(0, 2, 1), tile_mask, amplitudes, cholesky)
    ladder = pl.pallas_call(
        ladder_kernel,
        out_shape=jax.ShapeDtypeStruct((DV, DV), jnp.float32),
        in_specs=[vmem, vmem],
        out_specs=vmem,
        scratch_shapes=[
            pltpu.VMEM((RING, PACK, HT), half),
            pltpu.VMEM((RING, PACK, HT), half),
            pltpu.VMEM((2, PACK, HT), half),
            pltpu.VMEM((2 * RING, DV, DV), half),
            pltpu.VMEM((2, 2, DV, TILE), half),
            pltpu.VMEM((DV, DV), half),
            pltpu.VMEM((2, DV, DV), jnp.float32),
            pltpu.VMEM((SENDS, PART, DV), half),
            pltpu.VMEM((SENDS, PART, DV), half),
            pltpu.VMEM((SENDS, PART, DV), half),
            pltpu.VMEM((SENDS, PART, DV), half),
            dma((RING,)), dma((RING,)), dma((2,)), dma((RING,)), dma((2,)), dma((2,)), dma((2, 2)), dma((2, 2)),
            dma((SENDS,)), dma((SENDS,)), dma((SENDS,)), dma((SENDS,)),
        ],
        compiler_params=pltpu.CompilerParams(
            collective_id=0, has_side_effects=True, vmem_limit_bytes=36 << 20
        ),
        name="ladder",
    )(pack, weighted)
    return ladder.reshape(1, 1, DV, DV)


def solution(mesh):
    return jax.shard_map(
        shards,
        mesh=mesh,
        in_specs=(
            P("orow", "ocol", None, None),
            P("orow", "ocol", None, None),
            P(),
            P("ocol", None, None),
        ),
        out_specs=P("orow", "ocol", None, None),
        check_vma=False,
    )
```

```python
import jax
import jax.numpy as jnp
from jax import lax
from jax.experimental import pallas as pl
from jax.experimental.pallas import tpu as pltpu
from jax.sharding import PartitionSpec as P

TILE = 256
HT = 128
DV = 512
NO = 16
RING = 8
CHUNKS = 4
SENDS = 8
REST = 5
SOON = 4
LATE = 5
ROWS = DV // CHUNKS
PART = DV // SENDS
PACK = 8 * HT + 16
MESH = pl.DeviceIdType.MESH


def flip(index):
    return index + RING - 2 * RING * (index // RING)


def gives(i, j):
    even = (i // 4 + j // 4 + i + j) % 2 == 0
    return jnp.logical_or(jnp.logical_and(i > j, jnp.logical_not(even)), jnp.logical_and(i < j, even))


def leads(i, j):
    near = i // RING == j // RING
    return jnp.logical_or(
        jnp.logical_and(near, gives(i, j)), jnp.logical_and(jnp.logical_not(near), (i + j) % 2 == 0)
    )


def corner(shape=(HT, HT)):
    return lax.broadcasted_iota(jnp.int32, shape, 0), lax.broadcasted_iota(jnp.int32, shape, 1)


def prep_kernel(tiles_ref, mask_ref, amp_ref, chol_ref, pack_ref, weighted_ref, stage, raw, sems, raw_sem):
    i = lax.axis_index("orow")
    half = lax.axis_index("ocol") // RING
    raw_copy = pltpu.make_async_copy(amp_ref, raw, raw_sem)
    def pick(row, col, width, dst, sem):
        copy = pltpu.make_async_copy(
            chol_ref.at[0, pl.ds(pl.multiple_of(row, TILE), TILE), pl.ds(pl.multiple_of(col, HT), width)], dst, sem
        )
        copy.start()
        return copy

    copies, corners = [], []
    for s in range(RING + 1):
        if s < RING:
            j = half * RING + s
            other = jnp.logical_and(i // RING == half, gives(i, j))
            a = jnp.where(other, flip(i), i)
            b = jnp.where(other, flip(j), j)
        else:
            a = b = flip(i)
        t0 = tiles_ref[a, 0, b] * TILE
        t1 = tiles_ref[a, 1, b] * TILE

        mine = [pick(t, t, TILE, stage.at[s, n], sems.at[s, n]) for n, t in enumerate((t0, t1))]
        copies.append(mine)
        corners.append((t0, t1))
    raw_copy.start()
    for s, (t0, t1) in enumerate(corners):
        for n in range(2):
            copies[s].append(pick(t0, t1 + n * HT, HT, pack_ref.at[s, pl.ds(n * TILE, TILE)], sems.at[s, 2 + n]))
    row, col = corner()
    line = lax.broadcasted_iota(jnp.int32, (16, HT), 0)
    for s in range(RING + 1):
        ends = []
        for n in range(2):
            copies[s][n].wait()
            pack_ref[s, (4 + n) * HT : (5 + n) * HT, :] = stage[s, n, :HT, HT:]
            first = stage[s, n, :HT, :HT].astype(jnp.float32)
            second = stage[s, n, HT:, HT:].astype(jnp.float32)
            pack_ref[s, (6 + n) * HT : (7 + n) * HT, :] = jnp.where(row <= col, first, second).astype(jnp.bfloat16)
            ends.append(jnp.sum(jnp.where(row == col, second, 0.0), axis=0, keepdims=True))
        pack_ref[s, 8 * HT :, :] = jnp.where(line == 0, ends[0], ends[1]).astype(jnp.bfloat16)
    raw_copy.wait()
    for s in range(2):
        for t in range(2):
            keep = mask_ref[0, 0, s, t].astype(jnp.float32).astype(jnp.bfloat16)
            weighted_ref[t, pl.ds(s * TILE, TILE), :] = raw[0, 0, pl.ds(s * TILE, TILE), pl.ds(t * TILE, TILE)] * keep
    for s in range(RING + 1):
        for n in range(2, 4):
            copies[s][n].wait()


def ladder_kernel(
    pack_ref, weighted_ref, out_ref,
    slots, extra, through, factor, inputs, inner, total, give, got, pass_on, passed,
    f_send, f_recv, x_send, x_recv, r_send, r_recv, w_send, w_recv, p_send, p_recv, m_send, m_recv,
):
    i = lax.axis_index("orow")
    j = lax.axis_index("ocol")
    half = j // RING
    me = j - half * RING
    y, core = me // 2, me % 2
    fi, fj = flip(i), flip(j)
    same = i // RING == half
    diag = i == j
    lower = jnp.logical_and(same, gives(i, j))
    upper = jnp.logical_and(same, gives(j, i))
    not_lower = jnp.logical_not(lower)
    not_upper = jnp.logical_not(upper)
    swapped = jnp.logical_or(upper, diag)
    dflag = jnp.where(diag, 1, 0)
    w_dev = (jnp.where(swapped, fj, j), jnp.where(swapped, fi, i))
    p_swap = jnp.logical_or(lower, diag)
    p_dev = (jnp.where(p_swap, fj, j), jnp.where(p_swap, fi, i))
    m_dev = (fi, fj)
    t_dev = (j, i)

    def peer(k):
        step = k // 2
        dy = step + step // 2 - 2 * (step // 3)
        return ((y + dy) % 4) * 2 + (core + k) % 2

    entry = (i // 2) % 4
    ahead = entry % 2 == 0
    place = (y - entry + 4) % 4
    detours = jnp.logical_or(place == 0, place == jnp.where(ahead, 1, 3))
    relays = jnp.logical_not(detours)
    via = (y + jnp.where(jnp.logical_xor(place == 0, ahead), 1, 3)) % 4
    origin = (y + jnp.where(jnp.logical_xor(place == 2, ahead), 1, 3)) % 4

    barrier = pltpu.get_barrier_semaphore()

    def greet(device):
        pl.semaphore_signal(barrier, inc=1, device_id=device, device_id_type=MESH)

    for k in range(1, RING):
        greet((i, half * RING + peer(k)))
    greet(w_dev)

    @pl.when(jnp.logical_or(upper, lower))
    def _():
        greet(p_dev)

    @pl.when(lower)
    def _():
        greet(m_dev)

    pl.semaphore_wait(barrier, RING + jnp.where(diag, 0, jnp.where(same, 1, 0)) + jnp.where(lower, 1, 0))

    def remote(src, dst, send, recv, device):
        return pltpu.make_async_remote_copy(
            src_ref=src, dst_ref=dst, send_sem=send, recv_sem=recv, device_id=device, device_id_type=MESH
        )

    def w_copy(h):
        return remote(weighted_ref.at[h], inputs.at[1, h], w_send.at[1, h], w_recv.at[1, h], w_dev)

    def w_more(h):
        return remote(weighted_ref.at[h], inputs.at[0, h], w_send.at[0, h], w_recv.at[0, h], m_dev)

    def w_own(h):
        return pltpu.make_async_copy(weighted_ref.at[h], inputs.at[0, h], w_recv.at[0, h])

    lead = leads(i, j)
    w_first = jnp.logical_or(upper, jnp.logical_and(lead, jnp.logical_not(same)))
    w_held = jnp.logical_not(w_first)

    @pl.when(w_first)
    def _():
        for h in range(2):
            w_copy(h).start()

    for h in range(2):

        @pl.when(lower)
        def _():
            w_more(h).start()

        @pl.when(not_lower)
        def _():
            w_own(h).start()

    def leading(k):
        return leads(i, half * RING + peer(k))

    def f_copy(k):
        to = peer(k)
        return remote(pack_ref.at[to], slots.at[me], f_send.at[k], f_recv.at[me], (i, half * RING + to))

    def detour(n):
        to = peer(RING - 2 + n)
        return remote(
            pack_ref.at[to], through.at[n], f_send.at[RING - 2 + n], r_recv.at[n], (i, half * RING + via * 2 + core)
        )

    def forward(n):
        at = origin * 2 + core
        to = half * RING + (origin + 2) % 4 * 2 + (core + n) % 2
        return remote(through.at[n], slots.at[at], r_send.at[n], f_recv.at[at], (i, to))

    f_own = pltpu.make_async_copy(pack_ref.at[me], slots.at[me], f_send.at[0])
    f_own.start()
    x_copy = remote(pack_ref.at[RING], extra.at[me], x_send.at[0], x_recv.at[me], (i, i))
    x_own = pltpu.make_async_copy(pack_ref.at[RING], extra.at[me], x_send.at[1])
    def send_factors(first):
        for n in range(2):

            @pl.when(jnp.logical_and(detours, leading(RING - 2 + n) == first))
            def _():
                detour(n).start()

        for k in (6, 7, 2, 3, 4, 5, 1):

            @pl.when(jnp.logical_and(leading(k) == first, relays if k >= RING - 2 else True))
            def _():
                f_copy(k).start()

    send_factors(True)
    send_factors(False)

    @pl.when(jnp.logical_and(same, jnp.logical_not(diag)))
    def _():
        x_copy.start()

    @pl.when(diag)
    def _():
        x_own.start()

    total[...] = jnp.zeros_like(total)

    @pl.when(w_held)
    def _():
        for k in range(1, RING):

            @pl.when(leading(k))
            def _():
                f_copy(k).wait_send()

        for h in range(2):
            w_copy(h).start()

    @pl.when(not_lower)
    def _():
        for h in range(2):
            w_own(h).wait()

    f_own.wait()

    @pl.when(diag)
    def _():
        x_own.wait()

    row, col = corner()

    def build(source, slot, which):
        for n in range(2):
            at = n * TILE
            side = source[slot, 4 * HT + n * HT : 5 * HT + n * HT, :]
            mixed = source[slot, 6 * HT + n * HT : 7 * HT + n * HT, :].astype(jnp.float32)
            turned = mixed.T
            ends = source[slot, 8 * HT :, :].astype(jnp.float32)[n : n + 1, :]
            factor[which, at : at + HT, at : at + HT] = jnp.where(row <= col, mixed, turned).astype(jnp.bfloat16)
            factor[which, at : at + HT, at + HT : at + TILE] = side
            factor[which, at + HT : at + TILE, at : at + HT] = side.T
            factor[which, at + HT : at + TILE, at + HT : at + TILE] = jnp.where(
                row > col, mixed, jnp.where(row == col, ends, turned)
            ).astype(jnp.bfloat16)
            block = source[slot, n * TILE : n * TILE + TILE, :]
            factor[which, :TILE, TILE + n * HT : TILE + n * HT + HT] = block
            factor[which, TILE + n * HT : TILE + n * HT + HT, :TILE] = block.T

    def add(side, which):
        for h in range(2):
            inner[:, h * TILE : h * TILE + TILE] = jnp.dot(
                factor[which], inputs[side, h], preferred_element_type=jnp.float32
            ).astype(jnp.bfloat16)
        for c in range(2):
            cols = pl.ds(c * TILE, TILE)
            total[side, :, cols] += jnp.dot(
                inner[...], factor[which, :, cols], preferred_element_type=jnp.float32
            )

    def again(n, carry):
        add(1, n + RING * dflag)
        return carry

    def step(k, carry):
        slot = peer(k)

        @pl.when(k == LATE)
        def _():
            for h in range(2):
                w_copy(h).wait_recv()
            lax.fori_loop(0, LATE, again, 0)

        @pl.when(jnp.logical_and(lower, k == SOON))
        def _():
            for h in range(2):
                w_more(h).wait_recv()
            for n in range(SOON):
                add(0, n)

        for n in range(2):
            first = leads(i, half * RING + (origin + 2) % 4 * 2 + (core + n) % 2)

            @pl.when(jnp.logical_and(relays, k == jnp.where(first, 1, REST)))
            def _():
                detour(n).wait_recv()
                forward(n).start()

        @pl.when(k > 0)
        def _():
            remote(pack_ref.at[slot], slots.at[slot], f_send.at[slot], f_recv.at[slot], w_dev).wait_recv()

        build(slots, slot, k)

        @pl.when(diag)
        def _():
            @pl.when(k > 0)
            def _():
                remote(pack_ref.at[RING], extra.at[slot], x_send.at[0], x_recv.at[slot], w_dev).wait_recv()

            build(extra, slot, k + RING)

        @pl.when(jnp.logical_or(not_lower, k >= SOON))
        def _():
            add(0, k)

        lax.fori_loop(k, jnp.where(k < LATE, k, k + 1), again, 0)
        return carry

    lax.fori_loop(0, RING, step, 0)

    def p_copy(r):
        return remote(give.at[r], got.at[r], p_send.at[r], p_recv.at[r], p_dev)

    def m_copy(r):
        return remote(pass_on.at[r], passed.at[r], m_send.at[r], m_recv.at[r], t_dev)

    @pl.when(not_upper)
    def _():
        for r in range(CHUNKS):
            rows = pl.ds(r * ROWS, ROWS)
            ours = (total[1, rows, :] + total[dflag, :, rows].T).astype(jnp.bfloat16)
            for n in range(2):
                give[2 * r + n] = ours[n * PART : (n + 1) * PART]
                p_copy(2 * r + n).start()

    @pl.when(not_lower)
    def _():
        for r in range(CHUNKS):
            rows = pl.ds(r * ROWS, ROWS)
            out_ref[rows, :] = total[0, rows, :] + total[1 - dflag, :, rows].T
        for r in range(SENDS):
            rows = pl.ds(r * PART, PART)
            p_copy(r).wait_recv()
            ours = out_ref[rows, :] + got[r].astype(jnp.float32)
            out_ref[rows, :] = ours

            @pl.when(upper)
            def _():
                pass_on[r] = ours.astype(jnp.bfloat16)
                m_copy(r).start()

    @pl.when(lower)
    def _():
        for r in range(CHUNKS):
            for n in range(2):
                m_copy(2 * r + n).wait_recv()
            both = jnp.concatenate([passed[2 * r], passed[2 * r + 1]], axis=0)
            out_ref[:, pl.ds(r * ROWS, ROWS)] = both.astype(jnp.float32).T

    for h in range(2):
        w_copy(h).wait_send()
    for k in range(1, RING):

        @pl.when(jnp.logical_not(jnp.logical_and(w_held, leading(k))))
        def _():
            f_copy(k).wait_send()

    @pl.when(relays)
    def _():
        for n in range(2):
            forward(n).wait_send()

    @pl.when(not_upper)
    def _():
        for r in range(SENDS):
            p_copy(r).wait_send()

    @pl.when(upper)
    def _():
        for r in range(SENDS):
            m_copy(r).wait_send()

    @pl.when(jnp.logical_and(same, jnp.logical_not(diag)))
    def _():
        x_copy.wait_send()

    @pl.when(lower)
    def _():
        for h in range(2):
            w_more(h).wait_send()


def shards(amplitudes, tile_mask, domain_tiles, cholesky):
    vmem = pl.BlockSpec(memory_space=pltpu.VMEM)
    smem = pl.BlockSpec(memory_space=pltpu.SMEM)
    hbm = pl.BlockSpec(memory_space=pl.ANY)
    dma = pltpu.SemaphoreType.DMA
    half = jnp.bfloat16
    pack, weighted = pl.pallas_call(
        prep_kernel,
        out_shape=(
            pltpu.VMEM((RING + 1, PACK, HT), half),
            pltpu.VMEM((2, DV, TILE), half),
        ),
        in_specs=[smem, smem, hbm, hbm],
        out_specs=(vmem, vmem),
        scratch_shapes=[
            pltpu.VMEM((RING + 1, 2, TILE, TILE), half),
            pltpu.VMEM((1, 1, DV, DV), half),
            dma((RING + 1, 4)),
            dma,
        ],
        compiler_params=pltpu.CompilerParams(vmem_limit_bytes=56 << 20),
        name="prep",
    )(domain_tiles.transpose(0, 2, 1), tile_mask, amplitudes, cholesky)
    ladder = pl.pallas_call(
        ladder_kernel,
        out_shape=jax.ShapeDtypeStruct((DV, DV), jnp.float32),
        in_specs=[vmem, vmem],
        out_specs=vmem,
        scratch_shapes=[
            pltpu.VMEM((RING, PACK, HT), half),
            pltpu.VMEM((RING, PACK, HT), half),
            pltpu.VMEM((2, PACK, HT), half),
            pltpu.VMEM((2 * RING, DV, DV), half),
            pltpu.VMEM((2, 2, DV, TILE), half),
            pltpu.VMEM((DV, DV), half),
            pltpu.VMEM((2, DV, DV), jnp.float32),
            pltpu.VMEM((SENDS, PART, DV), half),
            pltpu.VMEM((SENDS, PART, DV), half),
            pltpu.VMEM((SENDS, PART, DV), half),
            pltpu.VMEM((SENDS, PART, DV), half),
            dma((RING,)), dma((RING,)), dma((2,)), dma((RING,)), dma((2,)), dma((2,)), dma((2, 2)), dma((2, 2)),
            dma((SENDS,)), dma((SENDS,)), dma((SENDS,)), dma((SENDS,)),
        ],
        compiler_params=pltpu.CompilerParams(
            collective_id=0, has_side_effects=True, vmem_limit_bytes=36 << 20
        ),
        name="ladder",
    )(pack, weighted)
    return ladder.reshape(1, 1, DV, DV)


def solution(mesh):
    return jax.shard_map(
        shards,
        mesh=mesh,
        in_specs=(
            P("orow", "ocol", None, None),
            P("orow", "ocol", None, None),
            P(),
            P("ocol", None, None),
        ),
        out_specs=P("orow", "ocol", None, None),
        check_vma=False,
    )
```
